128 devices in a mesh: req: 32 (over x, z_hi, y), tp: 4 (over z_lo, core).
Axes of the slice: x: 4, y: 4, z: 4 (z_hi: 2, z_lo: 2; z = z_hi * 2 + z_lo), core: 2. Of those that a mesh axis runs over, the one named last changes fastest.
Arguments:
- hidden_in: bfloat16 [12288, 1536], P('req', 'tp'), may hold values from -100 to 100
- norm_attn: float32 [1536], P('tp'), may hold values from 0.25 to 1.75
- w_query: bfloat16 [1536, 1536], P(None, 'tp'), may hold values from -0.15625 to 0.15625
- w_key: bfloat16 [1536, 256], replicated, may hold values from -0.3125 to 0.3125
- w_value: bfloat16 [1536, 256], replicated, may hold values from -0.15625 to 0.15625
- w_out: bfloat16 [1536, 1536], P('tp'), may hold values from -0.5 to 0.5
- prefix_cache: bfloat16 [512, 2, 2, 128, 128], P('req'), may hold values from -260 to 260
- page_table: int32 [8, 64], replicated, may hold values from 0 to 511, as said below
- group_of: int32 [32], replicated, may hold values from 0 to 7, as said below
- suffix_len: int32 [32], P('req'), may hold values from 96 to 384, as said below
- norm_moe: float32 [1536], P('tp'), may hold values from 0.25 to 1.75
- expert_ids: int32 [12288, 4], P('req'), may hold values from 0 to 31, all different within a row; in each aligned block of 384 rows (0 to 383, 384 to 767, ...) at most 72 rows name the same one
- expert_weights: float32 [12288, 4], P('req'), may hold values from 0.2 to 1
- w_gate: bfloat16 [32, 1536, 768], P('req', None, 'tp'), may hold values from -0.15625 to 0.15625
- w_up: bfloat16 [32, 1536, 768], P('req', None, 'tp'), may hold values from -0.15625 to 0.15625
- w_down: bfloat16 [32, 768, 1536], P('req', 'tp'), may hold values from -0.21875 to 0.21875
Outputs:
- layer_out: bfloat16 [12288, 1536], P('req', 'tp')
The draws below stay inside these ranges and needn't reach their ends.
Inputs may be any that keep to these rules, and one draw needn't show every extreme that they name: `page_table`: every page 0 to 511 appears exactly once; page p lies in row p // 16 of the req-sharded prefix_cache, in local slot p mod 16; every req index holds either none or exactly 4 pages of a prefix. `group_of`: every prefix serves exactly 4 requests. `suffix_len`: some request has exactly 384 suffix tokens. `expert_ids`: the 4 experts of a slot differ; in the 384 slots of one request no expert is named more than 72 times.
All inputs are finite; a program needn't handle non-finite values.
Results may differ from the reference program's by a relative error of at most 0.012.
The reference program's roundings to bfloat16 on the way count: a program that leaves them out, or rounds other values in their place, can miss the bound.
Values may be sent and summed in bfloat16 or wider, within the bound.
A program may use at most 128 MiB of HBM per device.

```python
import math
import jax
import jax.numpy as jnp
import numpy as np
from jax import lax

D = 1536
HEADS = 12
KVH = 2
HD = 128
FF = 768
TOP = 4
TOK_DEV = 384
PAGES_DEV = 16
PAGE = 128
REQ_GRP = 4
REQUESTS = 32
EXPERTS = 32
GROUPS = 8
PAGES_GRP = 64
PREFIX = 8192
PAGES_ALL = 512
PG_MOST = 4
CAP = 72
TOKENS = 12288
N_TP = 4


def draw_hidden_in(key, part):
    base_key = jax.random.fold_in(key, 11)
    key_rows, key_cols, key_vals = jax.random.split(base_key, 3)
    row_scale = jnp.exp(jax.random.uniform(key_rows, (TOKENS, 1), minval=math.log(0.3), maxval=math.log(3.0)))
    col_pos = jnp.arange(D).astype(jnp.float32)[None, :] / D
    col_rise = jnp.power(10.0, col_pos - 0.5)
    col_scale = jnp.exp(jax.random.uniform(key_cols, (1, D), minval=-0.35, maxval=0.35)) * col_rise
    values = jnp.clip(jax.random.normal(key_vals, (TOKENS, D)), -5.0, 5.0)
    return (values * row_scale * col_scale).astype(jnp.bfloat16)


def draw_prefix_cache(key, part):
    base_key = jax.random.fold_in(key, 23)
    key_vals = jax.random.fold_in(base_key, 0)
    shape_all = (PAGES_ALL, 2, KVH, PAGE, HD)
    is_key = (jnp.arange(2) == 0)[None, :, None, None, None]
    values = jnp.clip(jax.random.normal(key_vals, shape_all), -4.0, 4.0)
    values = values * jnp.where(is_key, 2.0, 1.0)
    return values.astype(jnp.bfloat16)


def draw_page_table(key, part):
    base_key = jax.random.fold_in(key, 37)
    key_owner, key_slot, key_order = jax.random.split(base_key, 3)
    owners = PAGES_ALL // PAGES_DEV
    tiles_dev = PAGES_DEV // PG_MOST
    tiles_group = owners * tiles_dev // GROUPS
    placing = jax.random.permutation(key_owner, owners)
    owner_at = jnp.argsort(placing)
    tile_ids = jnp.arange(GROUPS)[:, None] + GROUPS * jnp.arange(tiles_group)[None, :]
    tile_owner = owner_at[tile_ids // tiles_dev]
    tile_pos = tile_ids % tiles_dev
    slot_perm = jax.vmap(lambda sub_key: jax.random.permutation(sub_key, PAGES_DEV))(jax.random.split(key_slot, owners))
    slot_index = tile_pos[:, :, None] * PG_MOST + jnp.arange(PG_MOST)[None, None, :]
    slot_pick = slot_perm[tile_owner[:, :, None], slot_index]
    page_ids = (tile_owner[:, :, None] * PAGES_DEV + slot_pick).reshape(GROUPS, PAGES_GRP)
    page_order = jax.vmap(lambda sub_key: jax.random.permutation(sub_key, PAGES_GRP))(jax.random.split(key_order, GROUPS))
    return jnp.take_along_axis(page_ids, page_order, axis=1).astype(jnp.int32)


def draw_group_of(key, part):
    shuffled = jax.random.permutation(jax.random.fold_in(key, 41), REQUESTS)
    return (shuffled // REQ_GRP).astype(jnp.int32)


def draw_suffix_len(key, part):
    base_key = jax.random.fold_in(key, 53)
    key_kind, key_long, key_short, key_full = jax.random.split(base_key, 4)
    is_long = jax.random.randint(key_kind, (REQUESTS,), 0, 4) == 0
    long_len = jax.random.randint(key_long, (REQUESTS,), TOK_DEV // 2, TOK_DEV + 1)
    short_len = jax.random.randint(key_short, (REQUESTS,), max(1, TOK_DEV // 4), max(2, TOK_DEV // 2 + 1))
    lengths = jnp.where(is_long, long_len, short_len)
    full_one = jax.random.randint(key_full, (), 0, REQUESTS)
    lengths = jnp.where(jnp.arange(REQUESTS) == full_one, TOK_DEV, lengths)
    return lengths.astype(jnp.int32)


def levels(own_key, extent, shards, low, high):
    def one(position, shards_of):
        heights = jax.random.uniform(jax.random.fold_in(jax.random.fold_in(own_key, 6), position), (shards_of,), jnp.float32, low / len(shards), high / len(shards))
        return jnp.repeat(jnp.exp(heights), extent[position] // shards_of).reshape((-1,) + (1,) * (len(extent) - position - 1))

    loudness = one(*shards[0])
    for cut in shards[1:]:
        loudness = loudness * one(*cut)
    return loudness


def deal_out(own_key, own, number, rows, amount, top, reach, skew):
    ranking = jax.random.permutation(own_key, amount)
    heavy_load, common = portions_of(amount, rows * top, reach, skew, True), portions_of(amount, rows * top, reach, skew, False)
    places = jnp.arange(amount)

    def named(sizes, rotation):
        used = int((sizes > 0).sum())
        fixed = max(1, used // 4)
        moved = fixed + (places - fixed + rotation * (used - fixed)) % max(1, amount - fixed)
        return jnp.zeros((amount,), jnp.int32).at[ranking[jnp.where(places < fixed, places, moved)]].set(jnp.asarray(sizes, jnp.int32))

    sizes = jnp.where(number % 4 == 0, named(heavy_load, number // 4), named(common, number - number // 4 - 1))
    mixed = jax.random.permutation(jax.random.fold_in(own, 3), amount)
    donor, sink = mixed[0:amount // 2 * 2:2], mixed[1:amount // 2 * 2:2]
    slack = jnp.minimum(sizes[donor] - 1, reach - sizes[sink]) // 2
    slack = jnp.where((donor == ranking[0]) | (sink == ranking[0]) | (sizes[sink] == 0), 0, jnp.maximum(slack, 0))
    moved = jax.random.randint(jax.random.fold_in(own, 4), (amount // 2,), 0, 1 << 20) % (slack + 1)
    sizes = sizes.at[donor].add(-moved).at[sink].add(moved)
    labels = jnp.searchsorted(jnp.cumsum(sizes), jnp.arange(rows * top), side="right").astype(jnp.int32)
    table = labels.reshape(top, rows).T
    table = table[jax.random.permutation(jax.random.fold_in(own, 1), rows)]
    rotation = jax.random.randint(jax.random.fold_in(own, 2), (rows, 1), 0, top)
    return jnp.take_along_axis(table, (jnp.arange(top)[None, :] + rotation) % top, axis=1)


def portions_of(count, total, limit, lean, full):
    portions = [(1 << 20) // math.isqrt(grade ** lean) + 1 for grade in range(1, count + 1)]
    largest = limit if full else min(limit, max(-(-total // count), total * portions[0] // sum(portions)))
    least = 1 if total - largest >= count - 1 else 0
    counts, surplus = [largest] + [least] * (count - 1), total - largest - least * (count - 1)
    while surplus > 0:
        movable = [i for i in range(1, count) if counts[i] < largest] or [i for i in range(1, count) if counts[i] < limit]
        pool, left = sum([portions[i] for i in movable]), surplus
        for i in movable:
            extra = min(limit - counts[i], max(1, left * portions[i] // pool), surplus)
            counts[i] = counts[i] + extra
            surplus = surplus - extra
    return np.array(counts)


def gaussian(own_key, dims, scale, limit, shards=(), kind=jnp.bfloat16):
    drawn = jax.random.normal(own_key, dims, jnp.float32) * scale
    if len(shards) > 0:
        drawn = levels(own_key, dims, shards, -0.22, 0.18) * drawn
    return jnp.clip(drawn, min=-limit, max=limit).astype(kind)


def setup_inputs(seed: int = 0) -> dict:
    streams_of = jax.random.split(jax.random.key(seed), 17)
    hidden_in = draw_hidden_in(jax.random.fold_in(streams_of[16], 71), 0)
    norm_attn = jnp.clip(1.0 + 0.15 * jax.random.normal(streams_of[1], (D,), jnp.float32), 0.25, 1.75)
    w_query = gaussian(streams_of[2], (D, HEADS * HD), D ** -0.5, 0.15625, ((1, 4),))
    w_key = gaussian(streams_of[3], (D, KVH * HD), (D // 4) ** -0.5, 0.3125)
    w_value = gaussian(streams_of[4], (D, KVH * HD), D ** -0.5, 0.15625)
    w_out = gaussian(streams_of[5], (HEADS * HD, D), HD ** -0.5, 0.5, ((0, 4),))
    prefix_cache = draw_prefix_cache(jax.random.fold_in(streams_of[16], 71), 0)
    page_table = draw_page_table(jax.random.fold_in(streams_of[16], 71), 0)
    group_of = draw_group_of(jax.random.fold_in(streams_of[16], 71), 0)
    suffix_len = draw_suffix_len(jax.random.fold_in(streams_of[16], 71), 0)
    norm_moe = jnp.clip(1.0 + 0.15 * jax.random.normal(streams_of[10], (D,), jnp.float32), 0.25, 1.75)
    expert_ids_keys = jax.random.split(jax.random.fold_in(streams_of[11], 1), TOKENS // TOK_DEV)
    expert_ids_turns = jax.random.permutation(jax.random.fold_in(streams_of[11], 3), TOKENS // TOK_DEV)
    expert_ids = jax.vmap(lambda own, number: deal_out(jax.random.fold_in(streams_of[11], 2), own, number, TOK_DEV, EXPERTS, TOP, CAP, 2))(expert_ids_keys, expert_ids_turns).reshape((TOKENS, TOP))
    expert_weights = jnp.clip(0.2 + 0.8 * jax.random.uniform(streams_of[12], (TOKENS, TOP), jnp.float32) ** levels(streams_of[12], (TOKENS, TOP), ((0, 32),), -0.2, 0.2), 0.2, 1.0)
    w_gate = gaussian(streams_of[13], (EXPERTS, D, FF), D ** -0.5, 0.15625, ((0, 32), (2, 4)))
    w_up = gaussian(streams_of[14], (EXPERTS, D, FF), D ** -0.5, 0.15625, ((0, 32), (2, 4)))
    w_down = gaussian(streams_of[15], (EXPERTS, FF, D), FF ** -0.5, 0.21875, ((0, 32), (1, 4)))
    return dict(hidden_in=hidden_in, norm_attn=norm_attn, w_query=w_query, w_key=w_key, w_value=w_value, w_out=w_out, prefix_cache=prefix_cache, page_table=page_table, group_of=group_of, suffix_len=suffix_len, norm_moe=norm_moe, expert_ids=expert_ids, expert_weights=expert_weights, w_gate=w_gate, w_up=w_up, w_down=w_down)


EPSILON = 1e-06
ROPE_BASE = 1000000.0
MASKED = -1e+30

def rotate(values, positions):
    half_dim = values.shape[-1] // 2
    frequency = jnp.power(ROPE_BASE, -2.0 * jnp.arange(half_dim).astype(jnp.float32) / values.shape[-1])
    angles = positions[:, None] * frequency[None, :]
    cosine = jnp.cos(angles)[:, None, :]
    sine_part = jnp.sin(angles)[:, None, :]
    first_half = values[..., :half_dim]
    second = values[..., half_dim:]
    return jnp.concatenate([first_half * cosine - second * sine_part, second * cosine + first_half * sine_part], axis=-1)

def rms_scale(values):
    return lax.rsqrt(lax.optimization_barrier(jnp.mean(values * values, axis=-1, keepdims=True)) + EPSILON)

def attend_one(query_rows, key_suf, value_suf, group_cache):
    group_size = HEADS // KVH
    query_full = query_rows.astype(jnp.float32).reshape(TOK_DEV, KVH, group_size, HD)
    key_pre = jnp.transpose(group_cache[:, 0], (1, 0, 2, 3)).reshape(KVH, PREFIX, HD).astype(jnp.float32)
    value_pre = jnp.transpose(group_cache[:, 1], (1, 0, 2, 3)).reshape(KVH, PREFIX, HD).astype(jnp.float32)
    score_scale = 1.0 / math.sqrt(HD)
    scores_pre = jnp.einsum('tkgd,kpd->tkgp', query_full, key_pre) * score_scale
    scores_suf = jnp.einsum('tkgd,jkd->tkgj', query_full, key_suf.astype(jnp.float32)) * score_scale
    causal = jnp.arange(TOK_DEV)[:, None] >= jnp.arange(TOK_DEV)[None, :]
    scores_suf = jnp.where(causal[:, None, None, :], scores_suf, MASKED)
    row_max = jnp.maximum(lax.optimization_barrier(jnp.max(scores_pre, axis=-1)), lax.optimization_barrier(jnp.max(scores_suf, axis=-1)))[..., None]
    exp_pre = jnp.exp(scores_pre - row_max)
    exp_suf = jnp.exp(scores_suf - row_max)
    row_sum = lax.optimization_barrier(jnp.sum(exp_pre, axis=-1)) + lax.optimization_barrier(jnp.sum(exp_suf, axis=-1))
    weight_pre = lax.optimization_barrier(exp_pre.astype(jnp.bfloat16)).astype(jnp.float32)
    weight_suf = lax.optimization_barrier(exp_suf.astype(jnp.bfloat16)).astype(jnp.float32)
    weighted = jnp.einsum('tkgp,kpd->tkgd', weight_pre, value_pre)
    weighted = weighted + jnp.einsum('tkgj,jkd->tkgd', weight_suf, value_suf.astype(jnp.float32))
    return (weighted / row_sum[..., None]).astype(jnp.bfloat16).reshape(TOK_DEV, HEADS * HD)

def reference(hidden_in, norm_attn, w_query, w_key, w_value, w_out, prefix_cache, page_table, group_of, suffix_len, norm_moe, expert_ids, expert_weights, w_gate, w_up, w_down):
    hidden = hidden_in.astype(jnp.float32)
    normed = (hidden * rms_scale(hidden) * norm_attn).astype(jnp.bfloat16)
    positions = (PREFIX + jnp.arange(TOKENS) % TOK_DEV).astype(jnp.float32)
    query_lin = jnp.dot(normed, w_query, preferred_element_type=jnp.float32).reshape(TOKENS, HEADS, HD)
    key_lin = jnp.dot(normed, w_key, preferred_element_type=jnp.float32).reshape(TOKENS, KVH, HD)
    value_all = jnp.dot(normed, w_value, preferred_element_type=jnp.float32).astype(jnp.bfloat16).reshape(TOKENS, KVH, HD)
    query_all = rotate(query_lin, positions).astype(jnp.bfloat16)
    key_all = rotate(key_lin, positions).astype(jnp.bfloat16)

    def per_request(request_parts):
        query_rows, key_suf, value_suf, group_index = request_parts
        page_rows = lax.dynamic_index_in_dim(page_table, group_index, axis=0, keepdims=False)
        group_cache = jnp.take(prefix_cache, page_rows.astype(jnp.int32), axis=0)
        return attend_one(query_rows, key_suf, value_suf, group_cache)
    attention = lax.map(per_request, (query_all.reshape(REQUESTS, TOK_DEV, HEADS, HD), key_all.reshape(REQUESTS, TOK_DEV, KVH, HD), value_all.reshape(REQUESTS, TOK_DEV, KVH, HD), group_of))
    attention = attention.reshape(TOKENS, HEADS * HD)
    residual = hidden + jnp.dot(attention, w_out, preferred_element_type=jnp.float32)
    moe_in = (residual * rms_scale(residual) * norm_moe).astype(jnp.bfloat16)
    route_rows = expert_ids.reshape(REQUESTS, TOK_DEV * TOP)
    onehot_exp = (route_rows[:, :, None] == jnp.arange(EXPERTS).astype(jnp.int32)[None, None, :]).astype(jnp.int32)
    slot_rank = lax.optimization_barrier(jnp.sum(jnp.cumsum(onehot_exp, axis=1) * onehot_exp, axis=2)) - 1
    slot_global = (route_rows * (REQUESTS * CAP) + jnp.arange(REQUESTS).astype(jnp.int32)[:, None] * CAP + slot_rank).astype(jnp.int32)
    pair_token = (jnp.arange(TOKENS * TOP) // TOP).astype(jnp.int32)
    slot_table = jnp.zeros((EXPERTS * REQUESTS * CAP,), jnp.int32).at[slot_global.reshape(-1)].set(pair_token)
    quarter = FF // N_TP

    def per_expert(expert_parts):
        token_index, gate_mat, up_mat, down_mat = expert_parts
        rows_in = jnp.take(moe_in, token_index, axis=0)
        gate_lin = jnp.dot(rows_in, gate_mat, preferred_element_type=jnp.float32)
        up_lin = jnp.dot(rows_in, up_mat, preferred_element_type=jnp.float32)
        hidden_act = (jnp.maximum(gate_lin, 0.0) * up_lin).astype(jnp.bfloat16)
        down_parts = jnp.einsum('rqf,qfd->qrd', hidden_act.reshape(-1, N_TP, quarter).astype(jnp.float32), down_mat.reshape(N_TP, quarter, D).astype(jnp.float32))
        down_parts = lax.optimization_barrier(down_parts.astype(jnp.bfloat16)).astype(jnp.float32)
        return lax.optimization_barrier(jnp.sum(down_parts, axis=0)).astype(jnp.bfloat16)
    expert_out = lax.map(per_expert, (slot_table.reshape(EXPERTS, REQUESTS * CAP), w_gate, w_up, w_down))
    picked = jnp.take(expert_out.reshape(-1, D), slot_global.reshape(TOKENS, TOP), axis=0)
    moe_part = lax.optimization_barrier(jnp.sum(expert_weights[:, :, None] * picked.astype(jnp.float32), axis=1))
    layer_out = residual + moe_part
    live_rows = jnp.arange(TOKENS) % TOK_DEV < jnp.repeat(suffix_len, TOK_DEV)
    return jnp.where(live_rows[:, None], layer_out, 0.0).astype(jnp.bfloat16)
```

```python
import math

import jax
import jax.numpy as jnp
from jax import lax
from jax.sharding import PartitionSpec as P

D = 1536
KVH = 2
HD = 128
TOP = 4
PREFIX = 8192


EPSILON = 1e-06
ROPE_BASE = 1000000.0
MASKED = -1e30


def rotate(values, positions):
    half_dim = values.shape[-1] // 2
    frequency = jnp.power(
        ROPE_BASE, -2.0 * jnp.arange(half_dim).astype(jnp.float32) / values.shape[-1]
    )
    angles = positions[:, None] * frequency[None, :]
    cosine = jnp.cos(angles)[:, None, :]
    sine_part = jnp.sin(angles)[:, None, :]
    first_half = values[..., :half_dim]
    second = values[..., half_dim:]
    return jnp.concatenate(
        [first_half * cosine - second * sine_part, second * cosine + first_half * sine_part],
        axis=-1,
    )


def body(
    hidden_in,
    norm_attn,
    w_query,
    w_key,
    w_value,
    w_out,
    prefix_cache,
    page_table,
    group_of,
    suffix_len,
    norm_moe,
    expert_ids,
    expert_weights,
    w_gate,
    w_up,
    w_down,
):
    req_count = lax.axis_size("req")
    tp_count = lax.axis_size("tp")
    req_index = lax.axis_index("req")
    tp_index = lax.axis_index("tp")
    rows_here = hidden_in.shape[0]
    feature_cols = hidden_in.shape[1]
    heads_here = w_query.shape[1] // HD
    shared_head = tp_index // (tp_count // KVH)
    hidden = hidden_in.astype(jnp.float32)
    full_in = lax.all_gather(hidden_in, "tp", axis=1, tiled=True).astype(jnp.float32)
    sq_in = jnp.sum(full_in * full_in, axis=1)
    shard_piece = (full_in * lax.rsqrt(sq_in / D + EPSILON)[:, None] * norm_attn).astype(
        jnp.bfloat16
    )
    key_cols = lax.dynamic_slice_in_dim(w_key, shared_head * HD, HD, 1)
    value_cols = lax.dynamic_slice_in_dim(w_value, shared_head * HD, HD, 1)
    w_both = jnp.concatenate([key_cols, value_cols], axis=1)
    query_lin = jnp.dot(shard_piece, w_query, preferred_element_type=jnp.float32)
    pair_lin = jnp.dot(shard_piece, w_both, preferred_element_type=jnp.float32)
    positions = (PREFIX + jnp.arange(rows_here)).astype(jnp.float32)
    query_rot = rotate(query_lin.reshape(rows_here, heads_here, HD), positions).astype(jnp.bfloat16)
    key_suf = rotate(pair_lin[:, None, :HD], positions)[:, 0].astype(jnp.bfloat16)
    value_suf = pair_lin[:, HD:].astype(jnp.bfloat16)
    groups = page_table.shape[0]
    local_pages = prefix_cache.shape[0]
    page_rows = prefix_cache.shape[3]
    most_pages = min(local_pages // 2, 2 * page_table.shape[1] // req_count)
    my_group = group_of[req_index]
    owner_of = page_table // local_pages
    slot_of = page_table % local_pages
    owned_here = (owner_of == req_index).astype(jnp.int32)
    slot_rank = jnp.cumsum(owned_here, axis=1) - 1
    picker = (
        owned_here[:, :, None, None]
        * (slot_rank[:, :, None, None] == jnp.arange(most_pages)[None, None, :, None])
        * (slot_of[:, :, None, None] == jnp.arange(local_pages)[None, None, None, :])
    )
    picker = jnp.sum(picker, axis=1).astype(jnp.float32)
    peer_group = (group_of[:, None] == jnp.arange(groups)[None, :]).astype(jnp.float32)
    choose = jnp.einsum("qg,grs->qrs", peer_group, picker).astype(jnp.bfloat16)
    local_head = lax.dynamic_index_in_dim(prefix_cache, shared_head, axis=2, keepdims=False)
    flat_cache = local_head.reshape(local_pages, -1)
    outgoing = jnp.einsum(
        "qrs,sx->qrx", choose, flat_cache, preferred_element_type=jnp.float32
    ).astype(jnp.bfloat16)
    incoming = lax.all_to_all(
        outgoing.reshape(req_count, most_pages, 2, page_rows, HD),
        "req",
        split_axis=0,
        concat_axis=0,
        tiled=True,
    )
    keys_pre = incoming[:, :, 0]
    values_pre = incoming[:, :, 1]
    my_owners = lax.dynamic_index_in_dim(owner_of, my_group, axis=0, keepdims=False)
    page_count = jnp.sum(my_owners[None, :] == jnp.arange(req_count)[:, None], axis=1)
    live_slots = jnp.arange(most_pages)[None, :] < page_count[:, None]
    live_keys = jnp.broadcast_to(
        live_slots[:, :, None], (req_count, most_pages, page_rows)
    ).reshape(-1)
    key_total = req_count * most_pages * page_rows
    block_len = math.gcd(key_total, 2048)
    block_count = key_total // block_len
    score_scale = 1.0 / math.sqrt(HD)
    scores = (
        jnp.einsum("thd,jd->thj", query_rot, key_suf, preferred_element_type=jnp.float32)
        * score_scale
    )
    causal = jnp.arange(rows_here)[:, None] >= jnp.arange(rows_here)[None, :]
    scores = jnp.where(causal[:, None, :], scores, MASKED)
    row_max = jnp.max(scores, axis=2)
    weights = jnp.exp(scores - row_max[:, :, None])
    row_sum = jnp.sum(weights, axis=2)
    weighted = jnp.einsum(
        "thj,jd->thd", weights.astype(jnp.bfloat16), value_suf, preferred_element_type=jnp.float32
    )

    def absorb(running, block_parts):
        old_max, old_sum, old_weighted = running
        key_block, value_block, valid_block = block_parts
        block_scores = (
            jnp.einsum("thd,kd->thk", query_rot, key_block, preferred_element_type=jnp.float32)
            * score_scale
        )
        block_scores = jnp.where(valid_block[None, None, :], block_scores, MASKED)
        new_max = jnp.maximum(old_max, jnp.max(block_scores, axis=2))
        rescale = jnp.exp(old_max - new_max)
        block_weights = jnp.exp(block_scores - new_max[:, :, None])
        new_sum = old_sum * rescale + jnp.sum(block_weights, axis=2)
        new_weighted = old_weighted * rescale[:, :, None] + jnp.einsum(
            "thk,kd->thd",
            block_weights.astype(jnp.bfloat16),
            value_block,
            preferred_element_type=jnp.float32,
        )
        return ((new_max, new_sum, new_weighted), None)

    block_inputs = (
        keys_pre.reshape(block_count, block_len, HD),
        values_pre.reshape(block_count, block_len, HD),
        live_keys.reshape(block_count, block_len),
    )
    (row_max, row_sum, weighted), _ = lax.scan(absorb, (row_max, row_sum, weighted), block_inputs)
    attention = (
        (weighted / row_sum[:, :, None]).astype(jnp.bfloat16).reshape(rows_here, heads_here * HD)
    )
    proj_part = jnp.dot(attention, w_out, preferred_element_type=jnp.float32)
    attn_slice = lax.psum_scatter(
        proj_part.astype(jnp.bfloat16), "tp", scatter_dimension=1, tiled=True
    ).astype(jnp.float32)
    residual = hidden + attn_slice
    sq_mid = lax.psum(jnp.sum(residual * residual, axis=1), "tp")
    moe_in = (residual * lax.rsqrt(sq_mid / D + EPSILON)[:, None] * norm_moe).astype(jnp.bfloat16)
    expert_count = w_gate.shape[0] * req_count
    capacity = 3 * rows_here * TOP // (2 * expert_count)
    sub = capacity // tp_count
    gate_full = lax.all_gather(w_gate[0], "tp", axis=1, tiled=True)
    up_full = lax.all_gather(w_up[0], "tp", axis=1, tiled=True)
    down_full = lax.all_gather(w_down[0], "tp", axis=0, tiled=True)
    onehot_exp = (
        (expert_ids[:, :, None] == jnp.arange(expert_count)[None, None, :])
        .astype(jnp.int32)
        .reshape(rows_here * TOP, expert_count)
    )
    pair_rank = jnp.sum(jnp.cumsum(onehot_exp, axis=0) * onehot_exp, axis=1) - 1
    mine = (pair_rank // sub) == tp_index
    send_pos = expert_ids.reshape(-1) * sub + pair_rank % sub
    pair_token = jnp.arange(rows_here * TOP) // TOP
    slot_match = (send_pos[None, :] == jnp.arange(expert_count * sub)[:, None]) & mine[None, :]
    slot_token = jnp.sum(jnp.where(slot_match, pair_token[None, :], 0), axis=1)
    full_rows = lax.all_gather(moe_in, "tp", axis=1, tiled=True)
    outgoing_rows = jnp.take(full_rows, slot_token, axis=0).reshape(
        req_count, sub, full_rows.shape[1]
    )
    rows_in = lax.all_to_all(outgoing_rows, "req", split_axis=0, concat_axis=0, tiled=True)
    src_count, item_count, width_all = rows_in.shape
    flat_rows = rows_in.reshape(src_count * item_count, width_all)
    gate_lin = jnp.dot(flat_rows, gate_full, preferred_element_type=jnp.float32)
    up_lin = jnp.dot(flat_rows, up_full, preferred_element_type=jnp.float32)
    hidden_act = (jnp.maximum(gate_lin, 0.0) * up_lin).astype(jnp.bfloat16)
    block = hidden_act.shape[1] // tp_count
    down_parts = jnp.einsum(
        "rqf,qfd->qrd",
        hidden_act.reshape(-1, tp_count, block),
        down_full.reshape(tp_count, block, width_all),
        preferred_element_type=jnp.float32,
    ).astype(jnp.bfloat16)
    expert_out = jnp.sum(down_parts.astype(jnp.float32), axis=0).astype(jnp.bfloat16)
    returned = lax.all_to_all(
        expert_out.reshape(src_count, item_count, width_all),
        "req",
        split_axis=0,
        concat_axis=0,
        tiled=True,
    )
    flat_back = returned.reshape(-1, width_all)
    picked = jnp.take(flat_back, send_pos, axis=0).reshape(rows_here, TOP, width_all)
    pick_weight = jnp.where(mine.reshape(rows_here, TOP), expert_weights, 0.0)
    moe_full = jnp.sum(pick_weight[:, :, None] * picked.astype(jnp.float32), axis=1)
    moe_part = lax.psum_scatter(moe_full, "tp", scatter_dimension=1, tiled=True)
    layer_out = residual + moe_part
    live_rows = jnp.arange(rows_here) < suffix_len[0]
    return jnp.where(live_rows[:, None], layer_out, 0.0).astype(jnp.bfloat16)


def solution(mesh):
    in_specs = (
        P("req", "tp"),
        P(),
        P(None, "tp"),
        P(),
        P(),
        P("tp", None),
        P("req", None, None, None, None),
        P(),
        P(),
        P("req"),
        P("tp"),
        P("req", None),
        P("req", None),
        P("req", None, "tp"),
        P("req", None, "tp"),
        P("req", "tp", None),
    )
    out_specs = P("req", "tp")
    return jax.shard_map(body, mesh=mesh, in_specs=in_specs, out_specs=out_specs, check_vma=False)
```

```python
import math

import jax
import jax.numpy as jnp
from jax import lax
from jax.sharding import PartitionSpec as P

D = 1536
KVH = 2
HD = 128
TOP = 4
PREFIX = 8192


EPSILON = 1e-06
ROPE_BASE = 1000000.0
MASKED = -1e30


def rotate(values, positions):
    half_dim = values.shape[-1] // 2
    frequency = jnp.power(
        ROPE_BASE, -2.0 * jnp.arange(half_dim).astype(jnp.float32) / values.shape[-1]
    )
    angles = positions[:, None] * frequency[None, :]
    cosine = jnp.cos(angles)[:, None, :]
    sine_part = jnp.sin(angles)[:, None, :]
    first_half = values[..., :half_dim]
    second = values[..., half_dim:]
    return jnp.concatenate(
        [first_half * cosine - second * sine_part, second * cosine + first_half * sine_part],
        axis=-1,
    )


def body(
    hidden_in,
    norm_attn,
    w_query,
    w_key,
    w_value,
    w_out,
    prefix_cache,
    page_table,
    group_of,
    suffix_len,
    norm_moe,
    expert_ids,
    expert_weights,
    w_gate,
    w_up,
    w_down,
):
    req_count = lax.axis_size("req")
    tp_count = lax.axis_size("tp")
    req_index = lax.axis_index("req")
    tp_index = lax.axis_index("tp")
    rows_here = hidden_in.shape[0]
    feature_cols = hidden_in.shape[1]
    heads_here = w_query.shape[1] // HD
    shared_head = tp_index // (tp_count // KVH)
    hidden = hidden_in.astype(jnp.float32)
    full_in = lax.all_gather(hidden_in, "tp", axis=1, tiled=True).astype(jnp.float32)
    sq_in = jnp.sum(full_in * full_in, axis=1)
    shard_piece = (full_in * lax.rsqrt(sq_in / D + EPSILON)[:, None] * norm_attn).astype(
        jnp.bfloat16
    )
    key_cols = lax.dynamic_slice_in_dim(w_key, shared_head * HD, HD, 1)
    value_cols = lax.dynamic_slice_in_dim(w_value, shared_head * HD, HD, 1)
    w_both = jnp.concatenate([key_cols, value_cols], axis=1)
    query_lin = jnp.dot(shard_piece, w_query, preferred_element_type=jnp.float32)
    pair_lin = jnp.dot(shard_piece, w_both, preferred_element_type=jnp.float32)
    positions = (PREFIX + jnp.arange(rows_here)).astype(jnp.float32)
    query_rot = rotate(query_lin.reshape(rows_here, heads_here, HD), positions).astype(jnp.bfloat16)
    key_suf = rotate(pair_lin[:, None, :HD], positions)[:, 0].astype(jnp.bfloat16)
    value_suf = pair_lin[:, HD:].astype(jnp.bfloat16)
    groups = page_table.shape[0]
    local_pages = prefix_cache.shape[0]
    page_rows = prefix_cache.shape[3]
    most_pages = min(local_pages // 2, 2 * page_table.shape[1] // req_count)
    my_group = group_of[req_index]
    owner_of = page_table // local_pages
    slot_of = page_table % local_pages
    owned_here = (owner_of == req_index).astype(jnp.int32)
    slot_rank = jnp.cumsum(owned_here, axis=1) - 1
    picker = (
        owned_here[:, :, None, None]
        * (slot_rank[:, :, None, None] == jnp.arange(most_pages)[None, None, :, None])
        * (slot_of[:, :, None, None] == jnp.arange(local_pages)[None, None, None, :])
    )
    picker = jnp.sum(picker, axis=1).astype(jnp.float32)
    peer_group = (group_of[:, None] == jnp.arange(groups)[None, :]).astype(jnp.float32)
    choose = jnp.einsum("qg,grs->qrs", peer_group, picker).astype(jnp.bfloat16)
    pair_size = tp_count // KVH
    half_index = tp_index % pair_size
    half_rows = page_rows // pair_size
    local_head = lax.dynamic_index_in_dim(prefix_cache, shared_head, axis=2, keepdims=False)
    local_half = lax.dynamic_slice_in_dim(local_head, half_index * half_rows, half_rows, 2)
    flat_cache = local_half.reshape(local_pages, -1)
    outgoing = jnp.einsum(
        "qrs,sx->qrx", choose, flat_cache, preferred_element_type=jnp.float32
    ).astype(jnp.bfloat16)
    incoming = lax.all_to_all(
        outgoing.reshape(req_count, most_pages, 2, half_rows, HD),
        "req",
        split_axis=0,
        concat_axis=0,
        tiled=True,
    )
    my_owners = lax.dynamic_index_in_dim(owner_of, my_group, axis=0, keepdims=False)
    page_count = jnp.sum(my_owners[None, :] == jnp.arange(req_count)[:, None], axis=1)
    live_count = page_table.shape[1] // most_pages
    owner_live = page_count > 0
    live_rank = jnp.cumsum(owner_live.astype(jnp.int32)) - 1
    live_pick = (live_rank[None, :] == jnp.arange(live_count)[:, None]) & owner_live[None, :]
    live_owner = jnp.sum(jnp.where(live_pick, jnp.arange(req_count)[None, :], 0), axis=1)
    compact = jnp.take(incoming, live_owner, axis=0)
    keys_pre = compact[:, :, 0]
    values_pre = compact[:, :, 1]
    pair_perm = [(i, i ^ 1) for i in range(tp_count)]
    partner_query = lax.ppermute(query_rot, "tp", pair_perm)
    query_six = jnp.concatenate([query_rot, partner_query], axis=1)
    key_total = live_count * most_pages * half_rows
    block_len = math.gcd(key_total, 2048)
    block_count = key_total // block_len
    score_scale = 1.0 / math.sqrt(HD)
    scores = (
        jnp.einsum("thd,jd->thj", query_rot, key_suf, preferred_element_type=jnp.float32)
        * score_scale
    )
    causal = jnp.arange(rows_here)[:, None] >= jnp.arange(rows_here)[None, :]
    scores = jnp.where(causal[:, None, :], scores, MASKED)
    suf_max = jnp.max(scores, axis=2)
    weights = jnp.exp(scores - suf_max[:, :, None])
    suf_sum = jnp.sum(weights, axis=2)
    suf_weighted = jnp.einsum(
        "thj,jd->thd", weights.astype(jnp.bfloat16), value_suf, preferred_element_type=jnp.float32
    )

    def absorb(running, block_parts):
        old_max, old_sum, old_weighted = running
        key_block, value_block = block_parts
        block_scores = (
            jnp.einsum("thd,kd->thk", query_six, key_block, preferred_element_type=jnp.float32)
            * score_scale
        )
        new_max = jnp.maximum(old_max, jnp.max(block_scores, axis=2))
        rescale = jnp.exp(old_max - new_max)
        block_weights = jnp.exp(block_scores - new_max[:, :, None])
        new_sum = old_sum * rescale + jnp.sum(block_weights, axis=2)
        new_weighted = old_weighted * rescale[:, :, None] + jnp.einsum(
            "thk,kd->thd",
            block_weights.astype(jnp.bfloat16),
            value_block,
            preferred_element_type=jnp.float32,
        )
        return ((new_max, new_sum, new_weighted), None)

    block_inputs = (
        keys_pre.reshape(block_count, block_len, HD),
        values_pre.reshape(block_count, block_len, HD),
    )
    gate_full = lax.all_gather(w_gate[0], "tp", axis=1, tiled=True)
    up_full = lax.all_gather(w_up[0], "tp", axis=1, tiled=True)
    down_full = lax.all_gather(w_down[0], "tp", axis=0, tiled=True)
    gate_full, up_full, down_full, block_inputs = lax.optimization_barrier(
        (gate_full, up_full, down_full, block_inputs)
    )
    six = 2 * heads_here
    start_state = (
        jnp.full((rows_here, six), MASKED, jnp.float32),
        jnp.zeros((rows_here, six), jnp.float32),
        jnp.zeros((rows_here, six, HD), jnp.float32),
    )
    (pre_max, pre_sum, pre_weighted), _ = lax.scan(absorb, start_state, block_inputs)
    back = lax.ppermute(
        (pre_max[:, heads_here:], pre_sum[:, heads_here:], pre_weighted[:, heads_here:]),
        "tp",
        pair_perm,
    )
    parts = (
        (suf_max, suf_sum, suf_weighted),
        (pre_max[:, :heads_here], pre_sum[:, :heads_here], pre_weighted[:, :heads_here]),
        back,
    )
    row_max = jnp.maximum(jnp.maximum(parts[0][0], parts[1][0]), parts[2][0])
    row_sum = jnp.zeros_like(row_max)
    weighted = jnp.zeros_like(suf_weighted)
    for part_max, part_sum, part_weighted in parts:
        rescale = jnp.exp(part_max - row_max)
        row_sum = row_sum + part_sum * rescale
        weighted = weighted + part_weighted * rescale[:, :, None]
    attention = (
        (weighted / row_sum[:, :, None]).astype(jnp.bfloat16).reshape(rows_here, heads_here * HD)
    )
    proj_part = jnp.dot(attention, w_out, preferred_element_type=jnp.float32)
    attn_slice = lax.psum_scatter(
        proj_part.astype(jnp.bfloat16), "tp", scatter_dimension=1, tiled=True
    ).astype(jnp.float32)
    residual = hidden + attn_slice
    sq_mid = lax.psum(jnp.sum(residual * residual, axis=1), "tp")
    moe_in = (residual * lax.rsqrt(sq_mid / D + EPSILON)[:, None] * norm_moe).astype(jnp.bfloat16)
    expert_count = w_gate.shape[0] * req_count
    capacity = 3 * rows_here * TOP // (2 * expert_count)
    sub = capacity // tp_count
    onehot_exp = (
        (expert_ids[:, :, None] == jnp.arange(expert_count)[None, None, :])
        .astype(jnp.int32)
        .reshape(rows_here * TOP, expert_count)
    )
    pair_rank = jnp.sum(jnp.cumsum(onehot_exp, axis=0) * onehot_exp, axis=1) - 1
    mine = (pair_rank // sub) == tp_index
    send_pos = expert_ids.reshape(-1) * sub + pair_rank % sub
    pair_token = jnp.arange(rows_here * TOP) // TOP
    slot_match = (send_pos[None, :] == jnp.arange(expert_count * sub)[:, None]) & mine[None, :]
    slot_token = jnp.sum(jnp.where(slot_match, pair_token[None, :], 0), axis=1)
    full_rows = lax.all_gather(moe_in, "tp", axis=1, tiled=True)
    outgoing_rows = jnp.take(full_rows, slot_token, axis=0).reshape(
        req_count, sub, full_rows.shape[1]
    )
    rows_in = lax.all_to_all(outgoing_rows, "req", split_axis=0, concat_axis=0, tiled=True)
    src_count, item_count, width_all = rows_in.shape
    flat_rows = rows_in.reshape(src_count * item_count, width_all)
    gate_lin = jnp.dot(flat_rows, gate_full, preferred_element_type=jnp.float32)
    up_lin = jnp.dot(flat_rows, up_full, preferred_element_type=jnp.float32)
    hidden_act = (jnp.maximum(gate_lin, 0.0) * up_lin).astype(jnp.bfloat16)
    block = hidden_act.shape[1] // tp_count
    down_parts = jnp.einsum(
        "rqf,qfd->qrd",
        hidden_act.reshape(-1, tp_count, block),
        down_full.reshape(tp_count, block, width_all),
        preferred_element_type=jnp.float32,
    ).astype(jnp.bfloat16)
    expert_out = jnp.sum(down_parts.astype(jnp.float32), axis=0).astype(jnp.bfloat16)
    returned = lax.all_to_all(
        expert_out.reshape(src_count, item_count, width_all),
        "req",
        split_axis=0,
        concat_axis=0,
        tiled=True,
    )
    flat_back = returned.reshape(-1, width_all)
    picked = jnp.take(flat_back, send_pos, axis=0).reshape(rows_here, TOP, width_all)
    pick_weight = jnp.where(mine.reshape(rows_here, TOP), expert_weights, 0.0)
    moe_full = jnp.sum(pick_weight[:, :, None] * picked.astype(jnp.float32), axis=1)
    moe_part = lax.psum_scatter(moe_full, "tp", scatter_dimension=1, tiled=True)
    layer_out = residual + moe_part
    live_rows = jnp.arange(rows_here) < suffix_len[0]
    return jnp.where(live_rows[:, None], layer_out, 0.0).astype(jnp.bfloat16)


def solution(mesh):
    in_specs = (
        P("req", "tp"),
        P(),
        P(None, "tp"),
        P(),
        P(),
        P("tp", None),
        P("req", None, None, None, None),
        P(),
        P(),
        P("req"),
        P("tp"),
        P("req", None),
        P("req", None),
        P("req", None, "tp"),
        P("req", None, "tp"),
        P("req", "tp", None),
    )
    out_specs = P("req", "tp")
    return jax.shard_map(body, mesh=mesh, in_specs=in_specs, out_specs=out_specs, check_vma=False)
```

```python
import math

import jax
import jax.numpy as jnp
from jax import lax
from jax.sharding import PartitionSpec as P

D = 1536
KVH = 2
HD = 128
TOP = 4
PREFIX = 8192


EPSILON = 1e-06
ROPE_BASE = 1000000.0
MASKED = -1e30


def rotate(values, positions):
    half_dim = values.shape[-1] // 2
    frequency = jnp.power(
        ROPE_BASE, -2.0 * jnp.arange(half_dim).astype(jnp.float32) / values.shape[-1]
    )
    angles = positions[:, None] * frequency[None, :]
    cosine = jnp.cos(angles)[:, None, :]
    sine_part = jnp.sin(angles)[:, None, :]
    first_half = values[..., :half_dim]
    second = values[..., half_dim:]
    return jnp.concatenate(
        [first_half * cosine - second * sine_part, second * cosine + first_half * sine_part],
        axis=-1,
    )


def body(
    hidden_in,
    norm_attn,
    w_query,
    w_key,
    w_value,
    w_out,
    prefix_cache,
    page_table,
    group_of,
    suffix_len,
    norm_moe,
    expert_ids,
    expert_weights,
    w_gate,
    w_up,
    w_down,
):
    req_count = lax.axis_size("req")
    tp_count = lax.axis_size("tp")
    req_index = lax.axis_index("req")
    tp_index = lax.axis_index("tp")
    rows_here = hidden_in.shape[0]
    feature_cols = hidden_in.shape[1]
    heads_here = w_query.shape[1] // HD
    shared_head = tp_index // (tp_count // KVH)
    hidden = hidden_in.astype(jnp.float32)
    full_in = lax.all_gather(hidden_in, "tp", axis=1, tiled=True).astype(jnp.float32)
    sq_in = jnp.sum(full_in * full_in, axis=1)
    shard_piece = (full_in * lax.rsqrt(sq_in / D + EPSILON)[:, None] * norm_attn).astype(
        jnp.bfloat16
    )
    key_cols = lax.dynamic_slice_in_dim(w_key, shared_head * HD, HD, 1)
    value_cols = lax.dynamic_slice_in_dim(w_value, shared_head * HD, HD, 1)
    w_both = jnp.concatenate([key_cols, value_cols], axis=1)
    query_lin = jnp.dot(shard_piece, w_query, preferred_element_type=jnp.float32)
    pair_lin = jnp.dot(shard_piece, w_both, preferred_element_type=jnp.float32)
    positions = (PREFIX + jnp.arange(rows_here)).astype(jnp.float32)
    query_rot = rotate(query_lin.reshape(rows_here, heads_here, HD), positions).astype(jnp.bfloat16)
    key_suf = rotate(pair_lin[:, None, :HD], positions)[:, 0].astype(jnp.bfloat16)
    value_suf = pair_lin[:, HD:].astype(jnp.bfloat16)
    groups = page_table.shape[0]
    local_pages = prefix_cache.shape[0]
    page_rows = prefix_cache.shape[3]
    most_pages = min(local_pages // 2, 2 * page_table.shape[1] // req_count)
    my_group = group_of[req_index]
    owner_of = page_table // local_pages
    slot_of = page_table % local_pages
    owned_here = (owner_of == req_index).astype(jnp.int32)
    slot_rank = jnp.cumsum(owned_here, axis=1) - 1
    picker = (
        owned_here[:, :, None, None]
        * (slot_rank[:, :, None, None] == jnp.arange(most_pages)[None, None, :, None])
        * (slot_of[:, :, None, None] == jnp.arange(local_pages)[None, None, None, :])
    )
    picker = jnp.sum(picker, axis=1).astype(jnp.float32)
    peer_group = (group_of[:, None] == jnp.arange(groups)[None, :]).astype(jnp.float32)
    choose = jnp.einsum("qg,grs->qrs", peer_group, picker).astype(jnp.bfloat16)
    pair_size = tp_count // KVH
    half_index = tp_index % pair_size
    half_rows = page_rows // pair_size
    local_head = lax.dynamic_index_in_dim(prefix_cache, shared_head, axis=2, keepdims=False)
    local_half = lax.dynamic_slice_in_dim(local_head, half_index * half_rows, half_rows, 2)
    flat_cache = local_half.reshape(local_pages, -1)
    outgoing = jnp.einsum(
        "qrs,sx->qrx", choose, flat_cache, preferred_element_type=jnp.float32
    ).astype(jnp.bfloat16)
    incoming = lax.all_to_all(
        outgoing.reshape(req_count, most_pages, 2, half_rows, HD),
        "req",
        split_axis=0,
        concat_axis=0,
        tiled=True,
    )
    my_owners = lax.dynamic_index_in_dim(owner_of, my_group, axis=0, keepdims=False)
    page_count = jnp.sum(my_owners[None, :] == jnp.arange(req_count)[:, None], axis=1)
    live_count = page_table.shape[1] // most_pages
    owner_live = page_count > 0
    live_rank = jnp.cumsum(owner_live.astype(jnp.int32)) - 1
    live_pick = (live_rank[None, :] == jnp.arange(live_count)[:, None]) & owner_live[None, :]
    live_owner = jnp.sum(jnp.where(live_pick, jnp.arange(req_count)[None, :], 0), axis=1)
    compact = jnp.take(incoming, live_owner, axis=0)
    keys_pre = compact[:, :, 0]
    values_pre = compact[:, :, 1]
    pair_perm = [(i, i ^ 1) for i in range(tp_count)]
    partner_query = lax.ppermute(query_rot, "tp", pair_perm)
    query_six = jnp.concatenate([query_rot, partner_query], axis=1)
    key_total = live_count * most_pages * half_rows
    block_len = math.gcd(key_total, 2048)
    block_count = key_total // block_len
    score_scale = 1.0 / math.sqrt(HD)
    scores = (
        jnp.einsum("thd,jd->thj", query_rot, key_suf, preferred_element_type=jnp.float32)
        * score_scale
    )
    causal = jnp.arange(rows_here)[:, None] >= jnp.arange(rows_here)[None, :]
    scores = jnp.where(causal[:, None, :], scores, MASKED)
    suf_max = jnp.max(scores, axis=2)
    weights = jnp.exp(scores - suf_max[:, :, None])
    suf_sum = jnp.sum(weights, axis=2)
    suf_weighted = jnp.einsum(
        "thj,jd->thd", weights.astype(jnp.bfloat16), value_suf, preferred_element_type=jnp.float32
    )

    def absorb(running, block_parts):
        old_max, old_sum, old_weighted = running
        key_block, value_block = block_parts
        block_scores = (
            jnp.einsum("thd,kd->thk", query_six, key_block, preferred_element_type=jnp.float32)
            * score_scale
        )
        new_max = jnp.maximum(old_max, jnp.max(block_scores, axis=2))
        rescale = jnp.exp(old_max - new_max)
        block_weights = jnp.exp(block_scores - new_max[:, :, None])
        new_sum = old_sum * rescale + jnp.sum(block_weights, axis=2)
        new_weighted = old_weighted * rescale[:, :, None] + jnp.einsum(
            "thk,kd->thd",
            block_weights.astype(jnp.bfloat16),
            value_block,
            preferred_element_type=jnp.float32,
        )
        return ((new_max, new_sum, new_weighted), None)

    block_inputs = (
        keys_pre.reshape(block_count, block_len, HD),
        values_pre.reshape(block_count, block_len, HD),
    )
    gate_full = lax.all_gather(w_gate[0], "tp", axis=1, tiled=True)
    up_full = lax.all_gather(w_up[0], "tp", axis=1, tiled=True)
    down_full = lax.all_gather(w_down[0], "tp", axis=0, tiled=True)
    expert_count = w_gate.shape[0] * req_count
    capacity = 3 * rows_here * TOP // (2 * expert_count)
    sub = capacity // tp_count
    onehot_exp = (
        (expert_ids[:, :, None] == jnp.arange(expert_count)[None, None, :])
        .astype(jnp.int32)
        .reshape(rows_here * TOP, expert_count)
    )
    pair_rank = jnp.sum(jnp.cumsum(onehot_exp, axis=0) * onehot_exp, axis=1) - 1
    mine = (pair_rank // sub) == tp_index
    send_pos = expert_ids.reshape(-1) * sub + pair_rank % sub
    pair_token = jnp.arange(rows_here * TOP) // TOP
    slot_match = (send_pos[None, :] == jnp.arange(expert_count * sub)[:, None]) & mine[None, :]
    slot_token = jnp.sum(jnp.where(slot_match, pair_token[None, :], 0), axis=1)
    slot_token, send_pos, mine, block_inputs = lax.optimization_barrier(
        (slot_token, send_pos, mine, block_inputs)
    )
    six = 2 * heads_here
    start_state = (
        jnp.full((rows_here, six), MASKED, jnp.float32),
        jnp.zeros((rows_here, six), jnp.float32),
        jnp.zeros((rows_here, six, HD), jnp.float32),
    )
    (pre_max, pre_sum, pre_weighted), _ = lax.scan(absorb, start_state, block_inputs)
    gate_full, up_full, down_full, pre_max, pre_sum, pre_weighted = lax.optimization_barrier(
        (gate_full, up_full, down_full, pre_max, pre_sum, pre_weighted)
    )
    back = lax.ppermute(
        (pre_max[:, heads_here:], pre_sum[:, heads_here:], pre_weighted[:, heads_here:]),
        "tp",
        pair_perm,
    )
    parts = (
        (suf_max, suf_sum, suf_weighted),
        (pre_max[:, :heads_here], pre_sum[:, :heads_here], pre_weighted[:, :heads_here]),
        back,
    )
    row_max = jnp.maximum(jnp.maximum(parts[0][0], parts[1][0]), parts[2][0])
    row_sum = jnp.zeros_like(row_max)
    weighted = jnp.zeros_like(suf_weighted)
    for part_max, part_sum, part_weighted in parts:
        rescale = jnp.exp(part_max - row_max)
        row_sum = row_sum + part_sum * rescale
        weighted = weighted + part_weighted * rescale[:, :, None]
    attention = (
        (weighted / row_sum[:, :, None]).astype(jnp.bfloat16).reshape(rows_here, heads_here * HD)
    )
    proj_part = jnp.dot(attention, w_out, preferred_element_type=jnp.float32)
    attn_slice = lax.psum_scatter(
        proj_part.astype(jnp.bfloat16), "tp", scatter_dimension=1, tiled=True
    ).astype(jnp.float32)
    residual = hidden + attn_slice
    sq_mid = lax.psum(jnp.sum(residual * residual, axis=1), "tp")
    moe_in = (residual * lax.rsqrt(sq_mid / D + EPSILON)[:, None] * norm_moe).astype(jnp.bfloat16)
    full_rows = lax.all_gather(moe_in, "tp", axis=1, tiled=True)
    outgoing_rows = jnp.take(full_rows, slot_token, axis=0).reshape(
        req_count, sub, full_rows.shape[1]
    )
    rows_in = lax.all_to_all(outgoing_rows, "req", split_axis=0, concat_axis=0, tiled=True)
    src_count, item_count, width_all = rows_in.shape
    flat_rows = rows_in.reshape(src_count * item_count, width_all)
    gate_lin = jnp.dot(flat_rows, gate_full, preferred_element_type=jnp.float32)
    up_lin = jnp.dot(flat_rows, up_full, preferred_element_type=jnp.float32)
    hidden_act = (jnp.maximum(gate_lin, 0.0) * up_lin).astype(jnp.bfloat16)
    block = hidden_act.shape[1] // tp_count
    down_parts = jnp.einsum(
        "rqf,qfd->qrd",
        hidden_act.reshape(-1, tp_count, block),
        down_full.reshape(tp_count, block, width_all),
        preferred_element_type=jnp.float32,
    ).astype(jnp.bfloat16)
    expert_out = jnp.sum(down_parts.astype(jnp.float32), axis=0).astype(jnp.bfloat16)
    returned = lax.all_to_all(
        expert_out.reshape(src_count, item_count, width_all),
        "req",
        split_axis=0,
        concat_axis=0,
        tiled=True,
    )
    flat_back = returned.reshape(-1, width_all)
    picked = jnp.take(flat_back, send_pos, axis=0).reshape(rows_here, TOP, width_all)
    pick_weight = jnp.where(mine.reshape(rows_here, TOP), expert_weights, 0.0)
    moe_full = jnp.sum(pick_weight[:, :, None] * picked.astype(jnp.float32), axis=1)
    moe_part = lax.psum_scatter(moe_full, "tp", scatter_dimension=1, tiled=True)
    layer_out = residual + moe_part
    live_rows = jnp.arange(rows_here) < suffix_len[0]
    return jnp.where(live_rows[:, None], layer_out, 0.0).astype(jnp.bfloat16)


def solution(mesh):
    in_specs = (
        P("req", "tp"),
        P(),
        P(None, "tp"),
        P(),
        P(),
        P("tp", None),
        P("req", None, None, None, None),
        P(),
        P(),
        P("req"),
        P("tp"),
        P("req", None),
        P("req", None),
        P("req", None, "tp"),
        P("req", None, "tp"),
        P("req", "tp", None),
    )
    out_specs = P("req", "tp")
    return jax.shard_map(body, mesh=mesh, in_specs=in_specs, out_specs=out_specs, check_vma=False)
```

```python
import math

import jax
import jax.numpy as jnp
from jax import lax
from jax.sharding import PartitionSpec as P

D = 1536
KVH = 2
HD = 128
TOP = 4
PREFIX = 8192


EPSILON = 1e-06
ROPE_BASE = 1000000.0
MASKED = -1e30


def rotate(values, positions):
    half_dim = values.shape[-1] // 2
    frequency = jnp.power(
        ROPE_BASE, -2.0 * jnp.arange(half_dim).astype(jnp.float32) / values.shape[-1]
    )
    angles = positions[:, None] * frequency[None, :]
    cosine = jnp.cos(angles)[:, None, :]
    sine_part = jnp.sin(angles)[:, None, :]
    first_half = values[..., :half_dim]
    second = values[..., half_dim:]
    return jnp.concatenate(
        [first_half * cosine - second * sine_part, second * cosine + first_half * sine_part],
        axis=-1,
    )


def body(
    hidden_in,
    norm_attn,
    w_query,
    w_key,
    w_value,
    w_out,
    prefix_cache,
    page_table,
    group_of,
    suffix_len,
    norm_moe,
    expert_ids,
    expert_weights,
    w_gate,
    w_up,
    w_down,
):
    req_count = lax.axis_size("req")
    tp_count = lax.axis_size("tp")
    req_index = lax.axis_index("req")
    tp_index = lax.axis_index("tp")
    rows_here = hidden_in.shape[0]
    feature_cols = hidden_in.shape[1]
    heads_here = w_query.shape[1] // HD
    shared_head = tp_index // (tp_count // KVH)
    hidden = hidden_in.astype(jnp.float32)
    full_in = lax.all_gather(hidden_in, "tp", axis=1, tiled=True).astype(jnp.float32)
    sq_in = jnp.sum(full_in * full_in, axis=1)
    shard_piece = (full_in * lax.rsqrt(sq_in / D + EPSILON)[:, None] * norm_attn).astype(
        jnp.bfloat16
    )
    key_cols = lax.dynamic_slice_in_dim(w_key, shared_head * HD, HD, 1)
    value_cols = lax.dynamic_slice_in_dim(w_value, shared_head * HD, HD, 1)
    w_both = jnp.concatenate([key_cols, value_cols], axis=1)
    query_lin = jnp.dot(shard_piece, w_query, preferred_element_type=jnp.float32)
    pair_lin = jnp.dot(shard_piece, w_both, preferred_element_type=jnp.float32)
    positions = (PREFIX + jnp.arange(rows_here)).astype(jnp.float32)
    query_rot = rotate(query_lin.reshape(rows_here, heads_here, HD), positions).astype(jnp.bfloat16)
    key_suf = rotate(pair_lin[:, None, :HD], positions)[:, 0].astype(jnp.bfloat16)
    value_suf = pair_lin[:, HD:].astype(jnp.bfloat16)
    groups = page_table.shape[0]
    local_pages = prefix_cache.shape[0]
    page_rows = prefix_cache.shape[3]
    most_pages = min(local_pages // 2, 2 * page_table.shape[1] // req_count)
    my_group = group_of[req_index]
    owner_of = page_table // local_pages
    slot_of = page_table % local_pages
    owned_here = (owner_of == req_index).astype(jnp.int32)
    slot_rank = jnp.cumsum(owned_here, axis=1) - 1
    picker = (
        owned_here[:, :, None, None]
        * (slot_rank[:, :, None, None] == jnp.arange(most_pages)[None, None, :, None])
        * (slot_of[:, :, None, None] == jnp.arange(local_pages)[None, None, None, :])
    )
    picker = jnp.sum(picker, axis=1).astype(jnp.float32)
    peer_group = (group_of[:, None] == jnp.arange(groups)[None, :]).astype(jnp.float32)
    choose = jnp.einsum("qg,grs->qrs", peer_group, picker).astype(jnp.bfloat16)
    pair_size = tp_count // KVH
    half_index = tp_index % pair_size
    half_rows = page_rows // pair_size
    local_head = lax.dynamic_index_in_dim(prefix_cache, shared_head, axis=2, keepdims=False)
    local_half = lax.dynamic_slice_in_dim(local_head, half_index * half_rows, half_rows, 2)
    flat_cache = local_half.reshape(local_pages, -1)
    outgoing = jnp.einsum(
        "qrs,sx->qrx", choose, flat_cache, preferred_element_type=jnp.float32
    ).astype(jnp.bfloat16)
    incoming = lax.all_to_all(
        outgoing.reshape(req_count, most_pages, 2, half_rows, HD),
        "req",
        split_axis=0,
        concat_axis=0,
        tiled=True,
    )
    my_owners = lax.dynamic_index_in_dim(owner_of, my_group, axis=0, keepdims=False)
    page_count = jnp.sum(my_owners[None, :] == jnp.arange(req_count)[:, None], axis=1)
    live_count = page_table.shape[1] // most_pages
    owner_live = page_count > 0
    live_rank = jnp.cumsum(owner_live.astype(jnp.int32)) - 1
    live_pick = (live_rank[None, :] == jnp.arange(live_count)[:, None]) & owner_live[None, :]
    live_owner = jnp.sum(jnp.where(live_pick, jnp.arange(req_count)[None, :], 0), axis=1)
    compact = jnp.take(incoming, live_owner, axis=0)
    keys_pre = compact[:, :, 0]
    values_pre = compact[:, :, 1]
    pair_perm = [(i, i ^ 1) for i in range(tp_count)]
    partner_query = lax.ppermute(query_rot, "tp", pair_perm)
    query_six = jnp.concatenate([query_rot, partner_query], axis=1)
    key_total = live_count * most_pages * half_rows
    block_len = math.gcd(key_total, 2048)
    block_count = key_total // block_len
    score_scale = 1.0 / math.sqrt(HD)
    scores = (
        jnp.einsum("thd,jd->thj", query_rot, key_suf, preferred_element_type=jnp.float32)
        * score_scale
    )
    causal = jnp.arange(rows_here)[:, None] >= jnp.arange(rows_here)[None, :]
    scores = jnp.where(causal[:, None, :], scores, MASKED)
    suf_max = jnp.max(scores, axis=2)
    weights = jnp.exp(scores - suf_max[:, :, None])
    suf_sum = jnp.sum(weights, axis=2)
    suf_weighted = jnp.einsum(
        "thj,jd->thd", weights.astype(jnp.bfloat16), value_suf, preferred_element_type=jnp.float32
    )

    def absorb(running, block_parts):
        old_max, old_sum, old_weighted = running
        key_block, value_block = block_parts
        block_scores = (
            jnp.einsum("thd,kd->thk", query_six, key_block, preferred_element_type=jnp.float32)
            * score_scale
        )
        new_max = jnp.maximum(old_max, jnp.max(block_scores, axis=2))
        rescale = jnp.exp(old_max - new_max)
        block_weights = jnp.exp(block_scores - new_max[:, :, None])
        new_sum = old_sum * rescale + jnp.sum(block_weights, axis=2)
        new_weighted = old_weighted * rescale[:, :, None] + jnp.einsum(
            "thk,kd->thd",
            block_weights.astype(jnp.bfloat16),
            value_block,
            preferred_element_type=jnp.float32,
        )
        return ((new_max, new_sum, new_weighted), None)

    block_inputs = (
        keys_pre.reshape(block_count, block_len, HD),
        values_pre.reshape(block_count, block_len, HD),
    )
    gate_full = lax.all_gather(w_gate[0], "tp", axis=1, tiled=True)
    up_full = lax.all_gather(w_up[0], "tp", axis=1, tiled=True)
    down_full = lax.all_gather(w_down[0], "tp", axis=0, tiled=True)
    expert_count = w_gate.shape[0] * req_count
    capacity = 3 * rows_here * TOP // (2 * expert_count)
    sub = capacity // tp_count
    onehot_exp = (
        (expert_ids[:, :, None] == jnp.arange(expert_count)[None, None, :])
        .astype(jnp.int32)
        .reshape(rows_here * TOP, expert_count)
    )
    pair_rank = jnp.sum(jnp.cumsum(onehot_exp, axis=0) * onehot_exp, axis=1) - 1
    mine = (pair_rank // sub) == tp_index
    send_pos = expert_ids.reshape(-1) * sub + pair_rank % sub
    pair_token = jnp.arange(rows_here * TOP) // TOP
    slot_match = (send_pos[None, :] == jnp.arange(expert_count * sub)[:, None]) & mine[None, :]
    slot_token = jnp.sum(jnp.where(slot_match, pair_token[None, :], 0), axis=1)
    slot_token, send_pos, mine, block_inputs = lax.optimization_barrier(
        (slot_token, send_pos, mine, block_inputs)
    )
    six = 2 * heads_here
    start_state = (
        jnp.full((rows_here, six), MASKED, jnp.float32),
        jnp.zeros((rows_here, six), jnp.float32),
        jnp.zeros((rows_here, six, HD), jnp.float32),
    )
    (pre_max, pre_sum, pre_weighted), _ = lax.scan(absorb, start_state, block_inputs)
    gate_full, up_full, down_full, pre_max, pre_sum, pre_weighted = lax.optimization_barrier(
        (gate_full, up_full, down_full, pre_max, pre_sum, pre_weighted)
    )
    back = lax.ppermute(
        (pre_max[:, heads_here:], pre_sum[:, heads_here:], pre_weighted[:, heads_here:]),
        "tp",
        pair_perm,
    )
    parts = (
        (suf_max, suf_sum, suf_weighted),
        (pre_max[:, :heads_here], pre_sum[:, :heads_here], pre_weighted[:, :heads_here]),
        back,
    )
    row_max = jnp.maximum(jnp.maximum(parts[0][0], parts[1][0]), parts[2][0])
    row_sum = jnp.zeros_like(row_max)
    weighted = jnp.zeros_like(suf_weighted)
    for part_max, part_sum, part_weighted in parts:
        rescale = jnp.exp(part_max - row_max)
        row_sum = row_sum + part_sum * rescale
        weighted = weighted + part_weighted * rescale[:, :, None]
    attention = (
        (weighted / row_sum[:, :, None]).astype(jnp.bfloat16).reshape(rows_here, heads_here * HD)
    )
    proj_part = jnp.dot(attention, w_out, preferred_element_type=jnp.float32)
    attn_full = lax.psum(proj_part.astype(jnp.bfloat16), "tp").astype(jnp.float32)
    residual_full = full_in + attn_full
    sq_mid = jnp.sum(residual_full * residual_full, axis=1)
    full_rows = (residual_full * lax.rsqrt(sq_mid / D + EPSILON)[:, None] * norm_moe).astype(
        jnp.bfloat16
    )
    residual = lax.dynamic_slice_in_dim(residual_full, tp_index * feature_cols, feature_cols, 1)
    outgoing_rows = jnp.take(full_rows, slot_token, axis=0).reshape(
        req_count, sub, full_rows.shape[1]
    )
    rows_in = lax.all_to_all(outgoing_rows, "req", split_axis=0, concat_axis=0, tiled=True)
    src_count, item_count, width_all = rows_in.shape
    flat_rows = rows_in.reshape(src_count * item_count, width_all)
    gate_lin = jnp.dot(flat_rows, gate_full, preferred_element_type=jnp.float32)
    up_lin = jnp.dot(flat_rows, up_full, preferred_element_type=jnp.float32)
    hidden_act = (jnp.maximum(gate_lin, 0.0) * up_lin).astype(jnp.bfloat16)
    block = hidden_act.shape[1] // tp_count
    down_parts = jnp.einsum(
        "rqf,qfd->qrd",
        hidden_act.reshape(-1, tp_count, block),
        down_full.reshape(tp_count, block, width_all),
        preferred_element_type=jnp.float32,
    ).astype(jnp.bfloat16)
    expert_out = jnp.sum(down_parts.astype(jnp.float32), axis=0).astype(jnp.bfloat16)
    returned = lax.all_to_all(
        expert_out.reshape(src_count, item_count, width_all),
        "req",
        split_axis=0,
        concat_axis=0,
        tiled=True,
    )
    flat_back = returned.reshape(-1, width_all)
    pick_weight = jnp.where(mine.reshape(rows_here, TOP), expert_weights, 0.0)
    slot_hit = send_pos.reshape(rows_here, TOP)[:, :, None] == jnp.arange(flat_back.shape[0])
    combine = jnp.sum(jnp.where(slot_hit, pick_weight[:, :, None], 0.0), axis=1)
    moe_full = jnp.dot(
        combine,
        flat_back.astype(jnp.float32),
        precision=lax.Precision.HIGHEST,
        preferred_element_type=jnp.float32,
    )
    moe_part = lax.psum_scatter(moe_full, "tp", scatter_dimension=1, tiled=True)
    layer_out = residual + moe_part
    live_rows = jnp.arange(rows_here) < suffix_len[0]
    return jnp.where(live_rows[:, None], layer_out, 0.0).astype(jnp.bfloat16)


def solution(mesh):
    in_specs = (
        P("req", "tp"),
        P(),
        P(None, "tp"),
        P(),
        P(),
        P("tp", None),
        P("req", None, None, None, None),
        P(),
        P(),
        P("req"),
        P(),
        P("req", None),
        P("req", None),
        P("req", None, "tp"),
        P("req", None, "tp"),
        P("req", "tp", None),
    )
    out_specs = P("req", "tp")
    return jax.shard_map(body, mesh=mesh, in_specs=in_specs, out_specs=out_specs, check_vma=False)
```

```python
import math

import jax
import jax.numpy as jnp
from jax import lax
from jax.sharding import PartitionSpec as P

D = 1536
KVH = 2
HD = 128
TOP = 4
PREFIX = 8192


EPSILON = 1e-06
ROPE_BASE = 1000000.0
MASKED = -1e30


def rotate(values, positions):
    half_dim = values.shape[-1] // 2
    frequency = jnp.power(
        ROPE_BASE, -2.0 * jnp.arange(half_dim).astype(jnp.float32) / values.shape[-1]
    )
    angles = positions[:, None] * frequency[None, :]
    cosine = jnp.cos(angles)[:, None, :]
    sine_part = jnp.sin(angles)[:, None, :]
    first_half = values[..., :half_dim]
    second = values[..., half_dim:]
    return jnp.concatenate(
        [first_half * cosine - second * sine_part, second * cosine + first_half * sine_part],
        axis=-1,
    )


def body(
    hidden_in,
    norm_attn,
    w_query,
    w_key,
    w_value,
    w_out,
    prefix_cache,
    page_table,
    group_of,
    suffix_len,
    norm_moe,
    expert_ids,
    expert_weights,
    w_gate,
    w_up,
    w_down,
):
    req_count = lax.axis_size("req")
    tp_count = lax.axis_size("tp")
    req_index = lax.axis_index("req")
    tp_index = lax.axis_index("tp")
    rows_here = hidden_in.shape[0]
    feature_cols = hidden_in.shape[1]
    heads_here = w_query.shape[1] // HD
    shared_head = tp_index // (tp_count // KVH)
    hidden = hidden_in.astype(jnp.float32)
    full_in = lax.all_gather(hidden_in, "tp", axis=1, tiled=True).astype(jnp.float32)
    sq_in = jnp.sum(full_in * full_in, axis=1)
    shard_piece = (full_in * lax.rsqrt(sq_in / D + EPSILON)[:, None] * norm_attn).astype(
        jnp.bfloat16
    )
    key_cols = lax.dynamic_slice_in_dim(w_key, shared_head * HD, HD, 1)
    value_cols = lax.dynamic_slice_in_dim(w_value, shared_head * HD, HD, 1)
    w_both = jnp.concatenate([key_cols, value_cols], axis=1)
    query_lin = jnp.dot(shard_piece, w_query, preferred_element_type=jnp.float32)
    pair_lin = jnp.dot(shard_piece, w_both, preferred_element_type=jnp.float32)
    positions = (PREFIX + jnp.arange(rows_here)).astype(jnp.float32)
    query_rot = rotate(query_lin.reshape(rows_here, heads_here, HD), positions).astype(jnp.bfloat16)
    key_suf = rotate(pair_lin[:, None, :HD], positions)[:, 0].astype(jnp.bfloat16)
    value_suf = pair_lin[:, HD:].astype(jnp.bfloat16)
    groups = page_table.shape[0]
    local_pages = prefix_cache.shape[0]
    page_rows = prefix_cache.shape[3]
    most_pages = min(local_pages // 2, 2 * page_table.shape[1] // req_count)
    my_group = group_of[req_index]
    owner_of = page_table // local_pages
    slot_of = page_table % local_pages
    owned_here = (owner_of == req_index).astype(jnp.int32)
    slot_rank = jnp.cumsum(owned_here, axis=1) - 1
    picker = (
        owned_here[:, :, None, None]
        * (slot_rank[:, :, None, None] == jnp.arange(most_pages)[None, None, :, None])
        * (slot_of[:, :, None, None] == jnp.arange(local_pages)[None, None, None, :])
    )
    picker = jnp.sum(picker, axis=1).astype(jnp.float32)
    peer_group = (group_of[:, None] == jnp.arange(groups)[None, :]).astype(jnp.float32)
    choose = jnp.einsum("qg,grs->qrs", peer_group, picker).astype(jnp.bfloat16)
    pair_size = tp_count // KVH
    half_index = tp_index % pair_size
    half_rows = page_rows // pair_size
    local_head = lax.dynamic_index_in_dim(prefix_cache, shared_head, axis=2, keepdims=False)
    local_half = lax.dynamic_slice_in_dim(local_head, half_index * half_rows, half_rows, 2)
    flat_cache = local_half.reshape(local_pages, -1)
    outgoing = jnp.einsum(
        "qrs,sx->qrx", choose, flat_cache, preferred_element_type=jnp.float32
    ).astype(jnp.bfloat16)
    incoming = lax.all_to_all(
        outgoing.reshape(req_count, most_pages, 2, half_rows, HD),
        "req",
        split_axis=0,
        concat_axis=0,
        tiled=True,
    )
    my_owners = lax.dynamic_index_in_dim(owner_of, my_group, axis=0, keepdims=False)
    page_count = jnp.sum(my_owners[None, :] == jnp.arange(req_count)[:, None], axis=1)
    live_count = page_table.shape[1] // most_pages
    owner_live = page_count > 0
    live_rank = jnp.cumsum(owner_live.astype(jnp.int32)) - 1
    live_pick = (live_rank[None, :] == jnp.arange(live_count)[:, None]) & owner_live[None, :]
    live_owner = jnp.sum(jnp.where(live_pick, jnp.arange(req_count)[None, :], 0), axis=1)
    compact = jnp.take(incoming, live_owner, axis=0)
    keys_pre = compact[:, :, 0]
    values_pre = compact[:, :, 1]
    pair_perm = [(i, i ^ 1) for i in range(tp_count)]
    partner_query = lax.ppermute(query_rot, "tp", pair_perm)
    query_six = jnp.concatenate([query_rot, partner_query], axis=1)
    key_total = live_count * most_pages * half_rows
    block_len = math.gcd(key_total, 2048)
    block_count = key_total // block_len
    score_scale = 1.0 / math.sqrt(HD)
    scores = (
        jnp.einsum("thd,jd->thj", query_rot, key_suf, preferred_element_type=jnp.float32)
        * score_scale
    )
    causal = jnp.arange(rows_here)[:, None] >= jnp.arange(rows_here)[None, :]
    scores = jnp.where(causal[:, None, :], scores, MASKED)
    suf_max = jnp.max(scores, axis=2)
    weights = jnp.exp(scores - suf_max[:, :, None])
    suf_sum = jnp.sum(weights, axis=2)
    suf_weighted = jnp.einsum(
        "thj,jd->thd", weights.astype(jnp.bfloat16), value_suf, preferred_element_type=jnp.float32
    )

    def absorb(running, block_parts):
        old_max, old_sum, old_weighted = running
        key_block, value_block = block_parts
        block_scores = (
            jnp.einsum("thd,kd->thk", query_six, key_block, preferred_element_type=jnp.float32)
            * score_scale
        )
        new_max = jnp.maximum(old_max, jnp.max(block_scores, axis=2))
        rescale = jnp.exp(old_max - new_max)
        block_weights = jnp.exp(block_scores - new_max[:, :, None])
        new_sum = old_sum * rescale + jnp.sum(block_weights, axis=2)
        new_weighted = old_weighted * rescale[:, :, None] + jnp.einsum(
            "thk,kd->thd",
            block_weights.astype(jnp.bfloat16),
            value_block,
            preferred_element_type=jnp.float32,
        )
        return ((new_max, new_sum, new_weighted), None)

    block_inputs = (
        keys_pre.reshape(block_count, block_len, HD),
        values_pre.reshape(block_count, block_len, HD),
    )
    gate_full = lax.all_gather(w_gate[0], "tp", axis=1, tiled=True)
    up_full = lax.all_gather(w_up[0], "tp", axis=1, tiled=True)
    down_local, compact = lax.optimization_barrier((w_down[0], compact))
    down_stack = [down_local] + [
        lax.ppermute(down_local, "tp", [(i, (i + s) % tp_count) for i in range(tp_count)])
        for s in range(1, tp_count)
    ]
    down_order = (tp_index - jnp.arange(tp_count)) % tp_count
    down_full = jnp.take(jnp.stack(down_stack), down_order, axis=0).reshape(-1, D)
    expert_count = w_gate.shape[0] * req_count
    capacity = 3 * rows_here * TOP // (2 * expert_count)
    sub = capacity // tp_count
    onehot_exp = (
        (expert_ids[:, :, None] == jnp.arange(expert_count)[None, None, :])
        .astype(jnp.int32)
        .reshape(rows_here * TOP, expert_count)
    )
    pair_rank = jnp.sum(jnp.cumsum(onehot_exp, axis=0) * onehot_exp, axis=1) - 1
    mine = (pair_rank // sub) == tp_index
    send_pos = expert_ids.reshape(-1) * sub + pair_rank % sub
    pair_token = jnp.arange(rows_here * TOP) // TOP
    slot_match = (send_pos[None, :] == jnp.arange(expert_count * sub)[:, None]) & mine[None, :]
    slot_token = jnp.sum(jnp.where(slot_match, pair_token[None, :], 0), axis=1)
    slot_token, send_pos, mine, norm_moe, block_inputs = lax.optimization_barrier(
        (slot_token, send_pos, mine, norm_moe, block_inputs)
    )
    six = 2 * heads_here
    start_state = (
        jnp.full((rows_here, six), MASKED, jnp.float32),
        jnp.zeros((rows_here, six), jnp.float32),
        jnp.zeros((rows_here, six, HD), jnp.float32),
    )
    (pre_max, pre_sum, pre_weighted), _ = lax.scan(absorb, start_state, block_inputs)
    gate_full, up_full, down_full, pre_max, pre_sum, pre_weighted = lax.optimization_barrier(
        (gate_full, up_full, down_full, pre_max, pre_sum, pre_weighted)
    )
    back = lax.ppermute(
        (pre_max[:, heads_here:], pre_sum[:, heads_here:], pre_weighted[:, heads_here:]),
        "tp",
        pair_perm,
    )
    parts = (
        (suf_max, suf_sum, suf_weighted),
        (pre_max[:, :heads_here], pre_sum[:, :heads_here], pre_weighted[:, :heads_here]),
        back,
    )
    row_max = jnp.maximum(jnp.maximum(parts[0][0], parts[1][0]), parts[2][0])
    row_sum = jnp.zeros_like(row_max)
    weighted = jnp.zeros_like(suf_weighted)
    for part_max, part_sum, part_weighted in parts:
        rescale = jnp.exp(part_max - row_max)
        row_sum = row_sum + part_sum * rescale
        weighted = weighted + part_weighted * rescale[:, :, None]
    attention = (
        (weighted / row_sum[:, :, None]).astype(jnp.bfloat16).reshape(rows_here, heads_here * HD)
    )
    proj_part = jnp.dot(attention, w_out, preferred_element_type=jnp.float32)
    attn_full = lax.psum(proj_part.astype(jnp.bfloat16), "tp").astype(jnp.float32)
    residual_full = full_in + attn_full
    sq_mid = jnp.sum(residual_full * residual_full, axis=1)
    full_rows = (residual_full * lax.rsqrt(sq_mid / D + EPSILON)[:, None] * norm_moe).astype(
        jnp.bfloat16
    )
    residual = lax.dynamic_slice_in_dim(residual_full, tp_index * feature_cols, feature_cols, 1)
    outgoing_rows = jnp.take(full_rows, slot_token, axis=0).reshape(
        req_count, sub, full_rows.shape[1]
    )
    rows_in = lax.all_to_all(outgoing_rows, "req", split_axis=0, concat_axis=0, tiled=True)
    src_count, item_count, width_all = rows_in.shape
    flat_rows = rows_in.reshape(src_count * item_count, width_all)
    gate_lin = jnp.dot(flat_rows, gate_full, preferred_element_type=jnp.float32)
    up_lin = jnp.dot(flat_rows, up_full, preferred_element_type=jnp.float32)
    hidden_act = (jnp.maximum(gate_lin, 0.0) * up_lin).astype(jnp.bfloat16)
    block = hidden_act.shape[1] // tp_count
    down_parts = jnp.einsum(
        "rqf,qfd->qrd",
        hidden_act.reshape(-1, tp_count, block),
        down_full.reshape(tp_count, block, width_all),
        preferred_element_type=jnp.float32,
    ).astype(jnp.bfloat16)
    expert_out = jnp.sum(down_parts.astype(jnp.float32), axis=0).astype(jnp.bfloat16)
    returned = lax.all_to_all(
        expert_out.reshape(src_count, item_count, width_all),
        "req",
        split_axis=0,
        concat_axis=0,
        tiled=True,
    )
    flat_back = returned.reshape(-1, width_all)
    pick_weight = jnp.where(mine.reshape(rows_here, TOP), expert_weights, 0.0)
    slot_hit = send_pos.reshape(rows_here, TOP)[:, :, None] == jnp.arange(flat_back.shape[0])
    combine = jnp.sum(jnp.where(slot_hit, pick_weight[:, :, None], 0.0), axis=1)
    moe_full = jnp.dot(
        combine,
        flat_back.astype(jnp.float32),
        precision=lax.Precision.HIGHEST,
        preferred_element_type=jnp.float32,
    )
    moe_part = lax.psum_scatter(moe_full, "tp", scatter_dimension=1, tiled=True)
    layer_out = residual + moe_part
    live_rows = jnp.arange(rows_here) < suffix_len[0]
    return jnp.where(live_rows[:, None], layer_out, 0.0).astype(jnp.bfloat16)


def solution(mesh):
    in_specs = (
        P("req", "tp"),
        P(),
        P(None, "tp"),
        P(),
        P(),
        P("tp", None),
        P("req", None, None, None, None),
        P(),
        P(),
        P("req"),
        P(),
        P("req", None),
        P("req", None),
        P("req", None, "tp"),
        P("req", None, "tp"),
        P("req", "tp", None),
    )
    out_specs = P("req", "tp")
    return jax.shard_map(body, mesh=mesh, in_specs=in_specs, out_specs=out_specs, check_vma=False)
```

```python
import math

import jax
import jax.numpy as jnp
from jax import lax
from jax.sharding import PartitionSpec as P

D = 1536
KVH = 2
HD = 128
TOP = 4
PREFIX = 8192


EPSILON = 1e-06
ROPE_BASE = 1000000.0
MASKED = -1e30


def rotate(values, positions):
    half_dim = values.shape[-1] // 2
    frequency = jnp.power(
        ROPE_BASE, -2.0 * jnp.arange(half_dim).astype(jnp.float32) / values.shape[-1]
    )
    angles = positions[:, None] * frequency[None, :]
    cosine = jnp.cos(angles)[:, None, :]
    sine_part = jnp.sin(angles)[:, None, :]
    first_half = values[..., :half_dim]
    second = values[..., half_dim:]
    return jnp.concatenate(
        [first_half * cosine - second * sine_part, second * cosine + first_half * sine_part],
        axis=-1,
    )


def body(
    hidden_in,
    norm_attn,
    w_query,
    w_key,
    w_value,
    w_out,
    prefix_cache,
    page_table,
    group_of,
    suffix_len,
    norm_moe,
    expert_ids,
    expert_weights,
    w_gate,
    w_up,
    w_down,
):
    req_count = lax.axis_size("req")
    tp_count = lax.axis_size("tp")
    req_index = lax.axis_index("req")
    tp_index = lax.axis_index("tp")
    rows_here = hidden_in.shape[0]
    feature_cols = hidden_in.shape[1]
    heads_here = w_query.shape[1] // HD
    shared_head = tp_index // (tp_count // KVH)
    hidden = hidden_in.astype(jnp.float32)
    full_in = lax.all_gather(hidden_in, "tp", axis=1, tiled=True).astype(jnp.float32)
    sq_in = jnp.sum(full_in * full_in, axis=1)
    shard_piece = (full_in * lax.rsqrt(sq_in / D + EPSILON)[:, None] * norm_attn).astype(
        jnp.bfloat16
    )
    key_cols = lax.dynamic_slice_in_dim(w_key, shared_head * HD, HD, 1)
    value_cols = lax.dynamic_slice_in_dim(w_value, shared_head * HD, HD, 1)
    w_both = jnp.concatenate([key_cols, value_cols], axis=1)
    query_lin = jnp.dot(shard_piece, w_query, preferred_element_type=jnp.float32)
    pair_lin = jnp.dot(shard_piece, w_both, preferred_element_type=jnp.float32)
    positions = (PREFIX + jnp.arange(rows_here)).astype(jnp.float32)
    query_rot = rotate(query_lin.reshape(rows_here, heads_here, HD), positions).astype(jnp.bfloat16)
    key_suf = rotate(pair_lin[:, None, :HD], positions)[:, 0].astype(jnp.bfloat16)
    value_suf = pair_lin[:, HD:].astype(jnp.bfloat16)
    groups = page_table.shape[0]
    local_pages = prefix_cache.shape[0]
    page_rows = prefix_cache.shape[3]
    most_pages = min(local_pages // 2, 2 * page_table.shape[1] // req_count)
    my_group = group_of[req_index]
    owner_of = page_table // local_pages
    slot_of = page_table % local_pages
    owned_here = (owner_of == req_index).astype(jnp.int32)
    slot_rank = jnp.cumsum(owned_here, axis=1) - 1
    picker = (
        owned_here[:, :, None, None]
        * (slot_rank[:, :, None, None] == jnp.arange(most_pages)[None, None, :, None])
        * (slot_of[:, :, None, None] == jnp.arange(local_pages)[None, None, None, :])
    )
    picker = jnp.sum(picker, axis=1).astype(jnp.float32)
    peer_group = (group_of[:, None] == jnp.arange(groups)[None, :]).astype(jnp.float32)
    choose = jnp.einsum("qg,grs->qrs", peer_group, picker).astype(jnp.bfloat16)
    pair_size = tp_count // KVH
    half_index = tp_index % pair_size
    half_rows = page_rows // pair_size
    local_head = lax.dynamic_index_in_dim(prefix_cache, shared_head, axis=2, keepdims=False)
    local_half = lax.dynamic_slice_in_dim(local_head, half_index * half_rows, half_rows, 2)
    flat_cache = local_half.reshape(local_pages, -1)
    outgoing = jnp.einsum(
        "qrs,sx->qrx", choose, flat_cache, preferred_element_type=jnp.float32
    ).astype(jnp.bfloat16)
    incoming = lax.all_to_all(
        outgoing.reshape(req_count, most_pages, 2, half_rows, HD),
        "req",
        split_axis=0,
        concat_axis=0,
        tiled=True,
    )
    my_owners = lax.dynamic_index_in_dim(owner_of, my_group, axis=0, keepdims=False)
    page_count = jnp.sum(my_owners[None, :] == jnp.arange(req_count)[:, None], axis=1)
    live_count = page_table.shape[1] // most_pages
    owner_live = page_count > 0
    live_rank = jnp.cumsum(owner_live.astype(jnp.int32)) - 1
    live_pick = (live_rank[None, :] == jnp.arange(live_count)[:, None]) & owner_live[None, :]
    live_owner = jnp.sum(jnp.where(live_pick, jnp.arange(req_count)[None, :], 0), axis=1)
    compact = jnp.take(incoming, live_owner, axis=0)
    keys_pre = compact[:, :, 0]
    values_pre = compact[:, :, 1]
    pair_perm = [(i, i ^ 1) for i in range(tp_count)]
    partner_query = lax.ppermute(query_rot, "tp", pair_perm)
    query_six = jnp.concatenate([query_rot, partner_query], axis=1)
    key_total = live_count * most_pages * half_rows
    block_len = math.gcd(key_total, 2048)
    block_count = key_total // block_len
    score_scale = 1.0 / math.sqrt(HD)
    scores = (
        jnp.einsum("thd,jd->thj", query_rot, key_suf, preferred_element_type=jnp.float32)
        * score_scale
    )
    causal = jnp.arange(rows_here)[:, None] >= jnp.arange(rows_here)[None, :]
    scores = jnp.where(causal[:, None, :], scores, MASKED)
    suf_max = jnp.max(scores, axis=2)
    weights = jnp.exp(scores - suf_max[:, :, None])
    suf_sum = jnp.sum(weights, axis=2)
    suf_weighted = jnp.einsum(
        "thj,jd->thd", weights.astype(jnp.bfloat16), value_suf, preferred_element_type=jnp.float32
    )

    def absorb(running, block_parts):
        old_max, old_sum, old_weighted = running
        key_block, value_block = block_parts
        block_scores = (
            jnp.einsum("thd,kd->thk", query_six, key_block, preferred_element_type=jnp.float32)
            * score_scale
        )
        new_max = jnp.maximum(old_max, jnp.max(block_scores, axis=2))
        rescale = jnp.exp(old_max - new_max)
        block_weights = jnp.exp(block_scores - new_max[:, :, None])
        new_sum = old_sum * rescale + jnp.sum(block_weights, axis=2)
        new_weighted = old_weighted * rescale[:, :, None] + jnp.einsum(
            "thk,kd->thd",
            block_weights.astype(jnp.bfloat16),
            value_block,
            preferred_element_type=jnp.float32,
        )
        return ((new_max, new_sum, new_weighted), None)

    block_inputs = (
        keys_pre.reshape(block_count, block_len, HD),
        values_pre.reshape(block_count, block_len, HD),
    )
    gate_full = lax.all_gather(w_gate[0], "tp", axis=1, tiled=True)
    up_full = lax.all_gather(w_up[0], "tp", axis=1, tiled=True)
    expert_count = w_gate.shape[0] * req_count
    capacity = 3 * rows_here * TOP // (2 * expert_count)
    sub = capacity // tp_count
    onehot_exp = (
        (expert_ids[:, :, None] == jnp.arange(expert_count)[None, None, :])
        .astype(jnp.int32)
        .reshape(rows_here * TOP, expert_count)
    )
    pair_rank = jnp.sum(jnp.cumsum(onehot_exp, axis=0) * onehot_exp, axis=1) - 1
    mine = (pair_rank // sub) == tp_index
    send_pos = expert_ids.reshape(-1) * sub + pair_rank % sub
    pair_token = jnp.arange(rows_here * TOP) // TOP
    slot_match = (send_pos[None, :] == jnp.arange(expert_count * sub)[:, None]) & mine[None, :]
    slot_token = jnp.sum(jnp.where(slot_match, pair_token[None, :], 0), axis=1)
    slot_token, send_pos, mine, norm_moe, block_inputs = lax.optimization_barrier(
        (slot_token, send_pos, mine, norm_moe, block_inputs)
    )
    six = 2 * heads_here
    start_state = (
        jnp.full((rows_here, six), MASKED, jnp.float32),
        jnp.zeros((rows_here, six), jnp.float32),
        jnp.zeros((rows_here, six, HD), jnp.float32),
    )
    (pre_max, pre_sum, pre_weighted), _ = lax.scan(absorb, start_state, block_inputs)
    gate_full, up_full, pre_max, pre_sum, pre_weighted = lax.optimization_barrier(
        (gate_full, up_full, pre_max, pre_sum, pre_weighted)
    )
    back = lax.ppermute(
        (pre_max[:, heads_here:], pre_sum[:, heads_here:], pre_weighted[:, heads_here:]),
        "tp",
        pair_perm,
    )
    parts = (
        (suf_max, suf_sum, suf_weighted),
        (pre_max[:, :heads_here], pre_sum[:, :heads_here], pre_weighted[:, :heads_here]),
        back,
    )
    row_max = jnp.maximum(jnp.maximum(parts[0][0], parts[1][0]), parts[2][0])
    row_sum = jnp.zeros_like(row_max)
    weighted = jnp.zeros_like(suf_weighted)
    for part_max, part_sum, part_weighted in parts:
        rescale = jnp.exp(part_max - row_max)
        row_sum = row_sum + part_sum * rescale
        weighted = weighted + part_weighted * rescale[:, :, None]
    attention = (
        (weighted / row_sum[:, :, None]).astype(jnp.bfloat16).reshape(rows_here, heads_here * HD)
    )
    proj_part = jnp.dot(attention, w_out, preferred_element_type=jnp.float32)
    attn_sum = lax.psum(proj_part.astype(jnp.bfloat16), "tp")
    down_local, attn_sum = lax.optimization_barrier((w_down[0], attn_sum))
    down_full = lax.all_gather(down_local, "tp", axis=0, tiled=True)
    attn_full = attn_sum.astype(jnp.float32)
    residual_full = full_in + attn_full
    sq_mid = jnp.sum(residual_full * residual_full, axis=1)
    full_rows = (residual_full * lax.rsqrt(sq_mid / D + EPSILON)[:, None] * norm_moe).astype(
        jnp.bfloat16
    )
    residual = lax.dynamic_slice_in_dim(residual_full, tp_index * feature_cols, feature_cols, 1)
    outgoing_rows = jnp.take(full_rows, slot_token, axis=0).reshape(
        req_count, sub, full_rows.shape[1]
    )
    rows_in = lax.all_to_all(outgoing_rows, "req", split_axis=0, concat_axis=0, tiled=True)
    src_count, item_count, width_all = rows_in.shape
    flat_rows = rows_in.reshape(src_count * item_count, width_all)
    gate_lin = jnp.dot(flat_rows, gate_full, preferred_element_type=jnp.float32)
    up_lin = jnp.dot(flat_rows, up_full, preferred_element_type=jnp.float32)
    hidden_act = (jnp.maximum(gate_lin, 0.0) * up_lin).astype(jnp.bfloat16)
    block = hidden_act.shape[1] // tp_count
    down_parts = jnp.einsum(
        "rqf,qfd->qrd",
        hidden_act.reshape(-1, tp_count, block),
        down_full.reshape(tp_count, block, width_all),
        preferred_element_type=jnp.float32,
    ).astype(jnp.bfloat16)
    expert_out = jnp.sum(down_parts.astype(jnp.float32), axis=0).astype(jnp.bfloat16)
    returned = lax.all_to_all(
        expert_out.reshape(src_count, item_count, width_all),
        "req",
        split_axis=0,
        concat_axis=0,
        tiled=True,
    )
    flat_back = returned.reshape(-1, width_all)
    pick_weight = jnp.where(mine.reshape(rows_here, TOP), expert_weights, 0.0)
    slot_hit = send_pos.reshape(rows_here, TOP)[:, :, None] == jnp.arange(flat_back.shape[0])
    combine = jnp.sum(jnp.where(slot_hit, pick_weight[:, :, None], 0.0), axis=1)
    moe_full = jnp.dot(
        combine,
        flat_back.astype(jnp.float32),
        precision=lax.Precision.HIGHEST,
        preferred_element_type=jnp.float32,
    )
    moe_part = lax.psum_scatter(moe_full, "tp", scatter_dimension=1, tiled=True)
    layer_out = residual + moe_part
    live_rows = jnp.arange(rows_here) < suffix_len[0]
    return jnp.where(live_rows[:, None], layer_out, 0.0).astype(jnp.bfloat16)


def solution(mesh):
    in_specs = (
        P("req", "tp"),
        P(),
        P(None, "tp"),
        P(),
        P(),
        P("tp", None),
        P("req", None, None, None, None),
        P(),
        P(),
        P("req"),
        P(),
        P("req", None),
        P("req", None),
        P("req", None, "tp"),
        P("req", None, "tp"),
        P("req", "tp", None),
    )
    out_specs = P("req", "tp")
    return jax.shard_map(body, mesh=mesh, in_specs=in_specs, out_specs=out_specs, check_vma=False)
```

```python
import math

import jax
import jax.numpy as jnp
from jax import lax
from jax.sharding import PartitionSpec as P

D = 1536
KVH = 2
HD = 128
TOP = 4
PREFIX = 8192


EPSILON = 1e-06
ROPE_BASE = 1000000.0
MASKED = -1e30


def rotate(values, positions):
    half_dim = values.shape[-1] // 2
    frequency = jnp.power(
        ROPE_BASE, -2.0 * jnp.arange(half_dim).astype(jnp.float32) / values.shape[-1]
    )
    angles = positions[:, None] * frequency[None, :]
    cosine = jnp.cos(angles)[:, None, :]
    sine_part = jnp.sin(angles)[:, None, :]
    first_half = values[..., :half_dim]
    second = values[..., half_dim:]
    return jnp.concatenate(
        [first_half * cosine - second * sine_part, second * cosine + first_half * sine_part],
        axis=-1,
    )


def body(
    hidden_in,
    norm_attn,
    w_query,
    w_key,
    w_value,
    w_out,
    prefix_cache,
    page_table,
    group_of,
    suffix_len,
    norm_moe,
    expert_ids,
    expert_weights,
    w_gate,
    w_up,
    w_down,
):
    req_count = lax.axis_size("req")
    tp_count = lax.axis_size("tp")
    req_index = lax.axis_index("req")
    tp_index = lax.axis_index("tp")
    rows_here = hidden_in.shape[0]
    feature_cols = hidden_in.shape[1]
    heads_here = w_query.shape[1] // HD
    shared_head = tp_index // (tp_count // KVH)
    hidden = hidden_in.astype(jnp.float32)
    full_in = lax.all_gather(hidden_in, "tp", axis=1, tiled=True).astype(jnp.float32)
    sq_in = jnp.sum(full_in * full_in, axis=1)
    shard_piece = (full_in * lax.rsqrt(sq_in / D + EPSILON)[:, None] * norm_attn).astype(
        jnp.bfloat16
    )
    key_cols = lax.dynamic_slice_in_dim(w_key, shared_head * HD, HD, 1)
    value_cols = lax.dynamic_slice_in_dim(w_value, shared_head * HD, HD, 1)
    w_both = jnp.concatenate([key_cols, value_cols], axis=1)
    query_lin = jnp.dot(shard_piece, w_query, preferred_element_type=jnp.float32)
    pair_lin = jnp.dot(shard_piece, w_both, preferred_element_type=jnp.float32)
    positions = (PREFIX + jnp.arange(rows_here)).astype(jnp.float32)
    query_rot = rotate(query_lin.reshape(rows_here, heads_here, HD), positions).astype(jnp.bfloat16)
    key_suf = rotate(pair_lin[:, None, :HD], positions)[:, 0].astype(jnp.bfloat16)
    value_suf = pair_lin[:, HD:].astype(jnp.bfloat16)
    groups = page_table.shape[0]
    local_pages = prefix_cache.shape[0]
    page_rows = prefix_cache.shape[3]
    most_pages = min(local_pages // 2, 2 * page_table.shape[1] // req_count)
    my_group = group_of[req_index]
    owner_of = page_table // local_pages
    slot_of = page_table % local_pages
    owned_here = (owner_of == req_index).astype(jnp.int32)
    slot_rank = jnp.cumsum(owned_here, axis=1) - 1
    picker = (
        owned_here[:, :, None, None]
        * (slot_rank[:, :, None, None] == jnp.arange(most_pages)[None, None, :, None])
        * (slot_of[:, :, None, None] == jnp.arange(local_pages)[None, None, None, :])
    )
    picker = jnp.sum(picker, axis=1).astype(jnp.float32)
    peer_group = (group_of[:, None] == jnp.arange(groups)[None, :]).astype(jnp.float32)
    choose = jnp.einsum("qg,grs->qrs", peer_group, picker).astype(jnp.bfloat16)
    pair_size = tp_count // KVH
    half_index = tp_index % pair_size
    half_rows = page_rows // pair_size
    local_head = lax.dynamic_index_in_dim(prefix_cache, shared_head, axis=2, keepdims=False)
    local_half = lax.dynamic_slice_in_dim(local_head, half_index * half_rows, half_rows, 2)
    flat_cache = local_half.reshape(local_pages, -1)
    outgoing = jnp.einsum(
        "qrs,sx->qrx", choose, flat_cache, preferred_element_type=jnp.float32
    ).astype(jnp.bfloat16)
    incoming = lax.all_to_all(
        outgoing.reshape(req_count, most_pages, 2, half_rows, HD),
        "req",
        split_axis=0,
        concat_axis=0,
        tiled=True,
    )
    my_owners = lax.dynamic_index_in_dim(owner_of, my_group, axis=0, keepdims=False)
    page_count = jnp.sum(my_owners[None, :] == jnp.arange(req_count)[:, None], axis=1)
    live_count = page_table.shape[1] // most_pages
    owner_live = page_count > 0
    live_rank = jnp.cumsum(owner_live.astype(jnp.int32)) - 1
    live_pick = (live_rank[None, :] == jnp.arange(live_count)[:, None]) & owner_live[None, :]
    live_owner = jnp.sum(jnp.where(live_pick, jnp.arange(req_count)[None, :], 0), axis=1)
    compact = jnp.take(incoming, live_owner, axis=0)
    keys_pre = compact[:, :, 0]
    values_pre = compact[:, :, 1]
    pair_perm = [(i, i ^ 1) for i in range(tp_count)]
    partner_query = lax.ppermute(query_rot, "tp", pair_perm)
    query_six = jnp.concatenate([query_rot, partner_query], axis=1)
    key_total = live_count * most_pages * half_rows
    block_len = math.gcd(key_total, 2048)
    block_count = key_total // block_len
    score_scale = 1.0 / math.sqrt(HD)
    scores = (
        jnp.einsum("thd,jd->thj", query_rot, key_suf, preferred_element_type=jnp.float32)
        * score_scale
    )
    causal = jnp.arange(rows_here)[:, None] >= jnp.arange(rows_here)[None, :]
    scores = jnp.where(causal[:, None, :], scores, MASKED)
    suf_max = jnp.max(scores, axis=2)
    weights = jnp.exp(scores - suf_max[:, :, None])
    suf_sum = jnp.sum(weights, axis=2)
    suf_weighted = jnp.einsum(
        "thj,jd->thd", weights.astype(jnp.bfloat16), value_suf, preferred_element_type=jnp.float32
    )

    def absorb(running, block_parts):
        old_max, old_sum, old_weighted = running
        key_block, value_block = block_parts
        block_scores = (
            jnp.einsum("thd,kd->thk", query_six, key_block, preferred_element_type=jnp.float32)
            * score_scale
        )
        new_max = jnp.maximum(old_max, jnp.max(block_scores, axis=2))
        rescale = jnp.exp(old_max - new_max)
        block_weights = jnp.exp(block_scores - new_max[:, :, None])
        new_sum = old_sum * rescale + jnp.sum(block_weights, axis=2)
        new_weighted = old_weighted * rescale[:, :, None] + jnp.einsum(
            "thk,kd->thd",
            block_weights.astype(jnp.bfloat16),
            value_block,
            preferred_element_type=jnp.float32,
        )
        return ((new_max, new_sum, new_weighted), None)

    block_inputs = (
        keys_pre.reshape(block_count, block_len, HD),
        values_pre.reshape(block_count, block_len, HD),
    )
    gate_full = lax.all_gather(w_gate[0], "tp", axis=1, tiled=True)
    up_full = lax.all_gather(w_up[0], "tp", axis=1, tiled=True)
    expert_count = w_gate.shape[0] * req_count
    capacity = 3 * rows_here * TOP // (2 * expert_count)
    sub = capacity // tp_count
    onehot_exp = (
        (expert_ids[:, :, None] == jnp.arange(expert_count)[None, None, :])
        .astype(jnp.int32)
        .reshape(rows_here * TOP, expert_count)
    )
    pair_rank = jnp.sum(jnp.cumsum(onehot_exp, axis=0) * onehot_exp, axis=1) - 1
    mine = (pair_rank // sub) == tp_index
    send_pos = expert_ids.reshape(-1) * sub + pair_rank % sub
    pair_token = jnp.arange(rows_here * TOP) // TOP
    slot_match = (send_pos[None, :] == jnp.arange(expert_count * sub)[:, None]) & mine[None, :]
    slot_token = jnp.sum(jnp.where(slot_match, pair_token[None, :], 0), axis=1)
    slot_token, send_pos, mine, norm_moe, block_inputs = lax.optimization_barrier(
        (slot_token, send_pos, mine, norm_moe, block_inputs)
    )
    six = 2 * heads_here
    start_state = (
        jnp.full((rows_here, six), MASKED, jnp.float32),
        jnp.zeros((rows_here, six), jnp.float32),
        jnp.zeros((rows_here, six, HD), jnp.float32),
    )
    (pre_max, pre_sum, pre_weighted), _ = lax.scan(absorb, start_state, block_inputs)
    out_full = lax.all_gather(w_out, "tp", axis=0, tiled=True)
    gate_full, up_full, out_full, pre_max, pre_sum, pre_weighted = lax.optimization_barrier(
        (gate_full, up_full, out_full, pre_max, pre_sum, pre_weighted)
    )
    back = lax.ppermute(
        (pre_max[:, heads_here:], pre_sum[:, heads_here:], pre_weighted[:, heads_here:]),
        "tp",
        pair_perm,
    )
    parts = (
        (suf_max, suf_sum, suf_weighted),
        (pre_max[:, :heads_here], pre_sum[:, :heads_here], pre_weighted[:, :heads_here]),
        back,
    )
    row_max = jnp.maximum(jnp.maximum(parts[0][0], parts[1][0]), parts[2][0])
    row_sum = jnp.zeros_like(row_max)
    weighted = jnp.zeros_like(suf_weighted)
    for part_max, part_sum, part_weighted in parts:
        rescale = jnp.exp(part_max - row_max)
        row_sum = row_sum + part_sum * rescale
        weighted = weighted + part_weighted * rescale[:, :, None]
    attention = (
        (weighted / row_sum[:, :, None]).astype(jnp.bfloat16).reshape(rows_here, heads_here * HD)
    )
    attention_all = lax.all_gather(attention, "tp", axis=1, tiled=True)
    down_local, attention_all = lax.optimization_barrier((w_down[0], attention_all))
    down_full = lax.all_gather(down_local, "tp", axis=0, tiled=True)
    attn_full = jnp.dot(attention_all, out_full, preferred_element_type=jnp.float32)
    residual_full = full_in + attn_full
    sq_mid = jnp.sum(residual_full * residual_full, axis=1)
    full_rows = (residual_full * lax.rsqrt(sq_mid / D + EPSILON)[:, None] * norm_moe).astype(
        jnp.bfloat16
    )
    residual = lax.dynamic_slice_in_dim(residual_full, tp_index * feature_cols, feature_cols, 1)
    outgoing_rows = jnp.take(full_rows, slot_token, axis=0).reshape(
        req_count, sub, full_rows.shape[1]
    )
    rows_in = lax.all_to_all(outgoing_rows, "req", split_axis=0, concat_axis=0, tiled=True)
    src_count, item_count, width_all = rows_in.shape
    flat_rows = rows_in.reshape(src_count * item_count, width_all)
    gate_lin = jnp.dot(flat_rows, gate_full, preferred_element_type=jnp.float32)
    up_lin = jnp.dot(flat_rows, up_full, preferred_element_type=jnp.float32)
    hidden_act = (jnp.maximum(gate_lin, 0.0) * up_lin).astype(jnp.bfloat16)
    block = hidden_act.shape[1] // tp_count
    down_parts = jnp.einsum(
        "rqf,qfd->qrd",
        hidden_act.reshape(-1, tp_count, block),
        down_full.reshape(tp_count, block, width_all),
        preferred_element_type=jnp.float32,
    ).astype(jnp.bfloat16)
    expert_out = jnp.sum(down_parts.astype(jnp.float32), axis=0).astype(jnp.bfloat16)
    returned = lax.all_to_all(
        expert_out.reshape(src_count, item_count, width_all),
        "req",
        split_axis=0,
        concat_axis=0,
        tiled=True,
    )
    flat_back = returned.reshape(-1, width_all)
    pick_weight = jnp.where(mine.reshape(rows_here, TOP), expert_weights, 0.0)
    slot_hit = send_pos.reshape(rows_here, TOP)[:, :, None] == jnp.arange(flat_back.shape[0])
    combine = jnp.sum(jnp.where(slot_hit, pick_weight[:, :, None], 0.0), axis=1)
    moe_full = jnp.dot(
        combine,
        flat_back.astype(jnp.float32),
        precision=lax.Precision.HIGHEST,
        preferred_element_type=jnp.float32,
    )
    moe_part = lax.psum_scatter(moe_full, "tp", scatter_dimension=1, tiled=True)
    layer_out = residual + moe_part
    live_rows = jnp.arange(rows_here) < suffix_len[0]
    return jnp.where(live_rows[:, None], layer_out, 0.0).astype(jnp.bfloat16)


def solution(mesh):
    in_specs = (
        P("req", "tp"),
        P(),
        P(None, "tp"),
        P(),
        P(),
        P("tp", None),
        P("req", None, None, None, None),
        P(),
        P(),
        P("req"),
        P(),
        P("req", None),
        P("req", None),
        P("req", None, "tp"),
        P("req", None, "tp"),
        P("req", "tp", None),
    )
    out_specs = P("req", "tp")
    return jax.shard_map(body, mesh=mesh, in_specs=in_specs, out_specs=out_specs, check_vma=False)
```

```python
import math

import jax
import jax.numpy as jnp
from jax import lax
from jax.sharding import PartitionSpec as P

D = 1536
KVH = 2
HD = 128
TOP = 4
PREFIX = 8192


EPSILON = 1e-06
ROPE_BASE = 1000000.0
MASKED = -1e30


def rotate(values, positions):
    half_dim = values.shape[-1] // 2
    frequency = jnp.power(
        ROPE_BASE, -2.0 * jnp.arange(half_dim).astype(jnp.float32) / values.shape[-1]
    )
    angles = positions[:, None] * frequency[None, :]
    cosine = jnp.cos(angles)[:, None, :]
    sine_part = jnp.sin(angles)[:, None, :]
    first_half = values[..., :half_dim]
    second = values[..., half_dim:]
    return jnp.concatenate(
        [first_half * cosine - second * sine_part, second * cosine + first_half * sine_part],
        axis=-1,
    )


def body(
    hidden_in,
    norm_attn,
    w_query,
    w_key,
    w_value,
    w_out,
    prefix_cache,
    page_table,
    group_of,
    suffix_len,
    norm_moe,
    expert_ids,
    expert_weights,
    w_gate,
    w_up,
    w_down,
):
    req_count = lax.axis_size("req")
    tp_count = lax.axis_size("tp")
    req_index = lax.axis_index("req")
    tp_index = lax.axis_index("tp")
    rows_here = hidden_in.shape[0]
    feature_cols = hidden_in.shape[1]
    heads_here = w_query.shape[1] // HD
    shared_head = tp_index // (tp_count // KVH)
    hidden = hidden_in.astype(jnp.float32)
    full_in = lax.all_gather(hidden_in, "tp", axis=1, tiled=True).astype(jnp.float32)
    sq_in = jnp.sum(full_in * full_in, axis=1)
    shard_piece = (full_in * lax.rsqrt(sq_in / D + EPSILON)[:, None] * norm_attn).astype(
        jnp.bfloat16
    )
    key_cols = lax.dynamic_slice_in_dim(w_key, shared_head * HD, HD, 1)
    value_cols = lax.dynamic_slice_in_dim(w_value, shared_head * HD, HD, 1)
    w_both = jnp.concatenate([key_cols, value_cols], axis=1)
    query_lin = jnp.dot(shard_piece, w_query, preferred_element_type=jnp.float32)
    pair_lin = jnp.dot(shard_piece, w_both, preferred_element_type=jnp.float32)
    positions = (PREFIX + jnp.arange(rows_here)).astype(jnp.float32)
    query_rot = rotate(query_lin.reshape(rows_here, heads_here, HD), positions).astype(jnp.bfloat16)
    key_suf = rotate(pair_lin[:, None, :HD], positions)[:, 0].astype(jnp.bfloat16)
    value_suf = pair_lin[:, HD:].astype(jnp.bfloat16)
    groups = page_table.shape[0]
    local_pages = prefix_cache.shape[0]
    page_rows = prefix_cache.shape[3]
    most_pages = min(local_pages // 2, 2 * page_table.shape[1] // req_count)
    my_group = group_of[req_index]
    owner_of = page_table // local_pages
    slot_of = page_table % local_pages
    owned_here = (owner_of == req_index).astype(jnp.int32)
    slot_rank = jnp.cumsum(owned_here, axis=1) - 1
    picker = (
        owned_here[:, :, None, None]
        * (slot_rank[:, :, None, None] == jnp.arange(most_pages)[None, None, :, None])
        * (slot_of[:, :, None, None] == jnp.arange(local_pages)[None, None, None, :])
    )
    picker = jnp.sum(picker, axis=1).astype(jnp.float32)
    peer_group = (group_of[:, None] == jnp.arange(groups)[None, :]).astype(jnp.float32)
    choose = jnp.einsum("qg,grs->qrs", peer_group, picker).astype(jnp.bfloat16)
    pair_size = tp_count // KVH
    half_index = tp_index % pair_size
    half_rows = page_rows // pair_size
    local_head = lax.dynamic_index_in_dim(prefix_cache, shared_head, axis=2, keepdims=False)
    local_half = lax.dynamic_slice_in_dim(local_head, half_index * half_rows, half_rows, 2)
    flat_cache = local_half.reshape(local_pages, -1)
    outgoing = jnp.einsum(
        "qrs,sx->qrx", choose, flat_cache, preferred_element_type=jnp.float32
    ).astype(jnp.bfloat16)
    incoming = lax.all_to_all(
        outgoing.reshape(req_count, most_pages, 2, half_rows, HD),
        "req",
        split_axis=0,
        concat_axis=0,
        tiled=True,
    )
    my_owners = lax.dynamic_index_in_dim(owner_of, my_group, axis=0, keepdims=False)
    page_count = jnp.sum(my_owners[None, :] == jnp.arange(req_count)[:, None], axis=1)
    live_count = page_table.shape[1] // most_pages
    owner_live = page_count > 0
    live_rank = jnp.cumsum(owner_live.astype(jnp.int32)) - 1
    live_pick = (live_rank[None, :] == jnp.arange(live_count)[:, None]) & owner_live[None, :]
    live_owner = jnp.sum(jnp.where(live_pick, jnp.arange(req_count)[None, :], 0), axis=1)
    compact = jnp.take(incoming, live_owner, axis=0)
    keys_pre = compact[:, :, 0]
    values_pre = compact[:, :, 1]
    pair_perm = [(i, i ^ 1) for i in range(tp_count)]
    partner_query = lax.ppermute(query_rot, "tp", pair_perm)
    query_six = jnp.concatenate([query_rot, partner_query], axis=1)
    key_total = live_count * most_pages * half_rows
    block_len = math.gcd(key_total, 2048)
    block_count = key_total // block_len
    score_scale = 1.0 / math.sqrt(HD)
    scores = (
        jnp.einsum("thd,jd->thj", query_rot, key_suf, preferred_element_type=jnp.float32)
        * score_scale
    )
    causal = jnp.arange(rows_here)[:, None] >= jnp.arange(rows_here)[None, :]
    scores = jnp.where(causal[:, None, :], scores, MASKED)
    suf_max = jnp.max(scores, axis=2)
    weights = jnp.exp(scores - suf_max[:, :, None])
    suf_sum = jnp.sum(weights, axis=2)
    suf_weighted = jnp.einsum(
        "thj,jd->thd", weights.astype(jnp.bfloat16), value_suf, preferred_element_type=jnp.float32
    )

    def absorb(running, block_parts):
        old_max, old_sum, old_weighted = running
        key_block, value_block = block_parts
        block_scores = (
            jnp.einsum("thd,kd->thk", query_six, key_block, preferred_element_type=jnp.float32)
            * score_scale
        )
        new_max = jnp.maximum(old_max, jnp.max(block_scores, axis=2))
        rescale = jnp.exp(old_max - new_max)
        block_weights = jnp.exp(block_scores - new_max[:, :, None])
        new_sum = old_sum * rescale + jnp.sum(block_weights, axis=2)
        new_weighted = old_weighted * rescale[:, :, None] + jnp.einsum(
            "thk,kd->thd",
            block_weights.astype(jnp.bfloat16),
            value_block,
            preferred_element_type=jnp.float32,
        )
        return ((new_max, new_sum, new_weighted), None)

    block_inputs = (
        keys_pre.reshape(block_count, block_len, HD),
        values_pre.reshape(block_count, block_len, HD),
    )
    gate_full = lax.all_gather(w_gate[0], "tp", axis=1, tiled=True)
    expert_count = w_gate.shape[0] * req_count
    capacity = 3 * rows_here * TOP // (2 * expert_count)
    sub = capacity // tp_count
    onehot_exp = (
        (expert_ids[:, :, None] == jnp.arange(expert_count)[None, None, :])
        .astype(jnp.int32)
        .reshape(rows_here * TOP, expert_count)
    )
    pair_rank = jnp.sum(jnp.cumsum(onehot_exp, axis=0) * onehot_exp, axis=1) - 1
    mine = (pair_rank // sub) == tp_index
    send_pos = expert_ids.reshape(-1) * sub + pair_rank % sub
    pair_token = jnp.arange(rows_here * TOP) // TOP
    slot_match = (send_pos[None, :] == jnp.arange(expert_count * sub)[:, None]) & mine[None, :]
    slot_token = jnp.sum(jnp.where(slot_match, pair_token[None, :], 0), axis=1)
    slot_token, send_pos, mine, norm_moe, block_inputs = lax.optimization_barrier(
        (slot_token, send_pos, mine, norm_moe, block_inputs)
    )
    six = 2 * heads_here
    start_state = (
        jnp.full((rows_here, six), MASKED, jnp.float32),
        jnp.zeros((rows_here, six), jnp.float32),
        jnp.zeros((rows_here, six, HD), jnp.float32),
    )
    (pre_max, pre_sum, pre_weighted), _ = lax.scan(absorb, start_state, block_inputs)
    out_full = lax.all_gather(w_out, "tp", axis=0, tiled=True)
    gate_full, out_full, pre_max, pre_sum, pre_weighted = lax.optimization_barrier(
        (gate_full, out_full, pre_max, pre_sum, pre_weighted)
    )
    back = lax.ppermute(
        (pre_max[:, heads_here:], pre_sum[:, heads_here:], pre_weighted[:, heads_here:]),
        "tp",
        pair_perm,
    )
    parts = (
        (suf_max, suf_sum, suf_weighted),
        (pre_max[:, :heads_here], pre_sum[:, :heads_here], pre_weighted[:, :heads_here]),
        back,
    )
    row_max = jnp.maximum(jnp.maximum(parts[0][0], parts[1][0]), parts[2][0])
    row_sum = jnp.zeros_like(row_max)
    weighted = jnp.zeros_like(suf_weighted)
    for part_max, part_sum, part_weighted in parts:
        rescale = jnp.exp(part_max - row_max)
        row_sum = row_sum + part_sum * rescale
        weighted = weighted + part_weighted * rescale[:, :, None]
    attention = (
        (weighted / row_sum[:, :, None]).astype(jnp.bfloat16).reshape(rows_here, heads_here * HD)
    )
    attention_all = lax.all_gather(attention, "tp", axis=1, tiled=True)
    up_local, down_local, attention_all = lax.optimization_barrier(
        (w_up[0], w_down[0], attention_all)
    )
    up_full = lax.all_gather(up_local, "tp", axis=1, tiled=True)
    down_full = lax.all_gather(down_local, "tp", axis=0, tiled=True)
    attn_full = jnp.dot(attention_all, out_full, preferred_element_type=jnp.float32)
    residual_full = full_in + attn_full
    sq_mid = jnp.sum(residual_full * residual_full, axis=1)
    full_rows = (residual_full * lax.rsqrt(sq_mid / D + EPSILON)[:, None] * norm_moe).astype(
        jnp.bfloat16
    )
    residual = lax.dynamic_slice_in_dim(residual_full, tp_index * feature_cols, feature_cols, 1)
    outgoing_rows = jnp.take(full_rows, slot_token, axis=0).reshape(
        req_count, sub, full_rows.shape[1]
    )
    rows_in = lax.all_to_all(outgoing_rows, "req", split_axis=0, concat_axis=0, tiled=True)
    src_count, item_count, width_all = rows_in.shape
    flat_rows = rows_in.reshape(src_count * item_count, width_all)
    gate_lin = jnp.dot(flat_rows, gate_full, preferred_element_type=jnp.float32)
    up_lin = jnp.dot(flat_rows, up_full, preferred_element_type=jnp.float32)
    hidden_act = (jnp.maximum(gate_lin, 0.0) * up_lin).astype(jnp.bfloat16)
    block = hidden_act.shape[1] // tp_count
    down_parts = jnp.einsum(
        "rqf,qfd->qrd",
        hidden_act.reshape(-1, tp_count, block),
        down_full.reshape(tp_count, block, width_all),
        preferred_element_type=jnp.float32,
    ).astype(jnp.bfloat16)
    expert_out = jnp.sum(down_parts.astype(jnp.float32), axis=0).astype(jnp.bfloat16)
    returned = lax.all_to_all(
        expert_out.reshape(src_count, item_count, width_all),
        "req",
        split_axis=0,
        concat_axis=0,
        tiled=True,
    )
    flat_back = returned.reshape(-1, width_all)
    pick_weight = jnp.where(mine.reshape(rows_here, TOP), expert_weights, 0.0)
    slot_hit = send_pos.reshape(rows_here, TOP)[:, :, None] == jnp.arange(flat_back.shape[0])
    combine = jnp.sum(jnp.where(slot_hit, pick_weight[:, :, None], 0.0), axis=1)
    moe_full = jnp.dot(
        combine,
        flat_back.astype(jnp.float32),
        precision=lax.Precision.HIGHEST,
        preferred_element_type=jnp.float32,
    )
    moe_part = lax.psum_scatter(moe_full, "tp", scatter_dimension=1, tiled=True)
    layer_out = residual + moe_part
    live_rows = jnp.arange(rows_here) < suffix_len[0]
    return jnp.where(live_rows[:, None], layer_out, 0.0).astype(jnp.bfloat16)


def solution(mesh):
    in_specs = (
        P("req", "tp"),
        P(),
        P(None, "tp"),
        P(),
        P(),
        P("tp", None),
        P("req", None, None, None, None),
        P(),
        P(),
        P("req"),
        P(),
        P("req", None),
        P("req", None),
        P("req", None, "tp"),
        P("req", None, "tp"),
        P("req", "tp", None),
    )
    out_specs = P("req", "tp")
    return jax.shard_map(body, mesh=mesh, in_specs=in_specs, out_specs=out_specs, check_vma=False)
```

```python
import math

import jax
import jax.numpy as jnp
from jax import lax
from jax.sharding import PartitionSpec as P

D = 1536
KVH = 2
HD = 128
TOP = 4
PREFIX = 8192


EPSILON = 1e-06
ROPE_BASE = 1000000.0
MASKED = -1e30


def rotate(values, positions):
    half_dim = values.shape[-1] // 2
    frequency = jnp.power(
        ROPE_BASE, -2.0 * jnp.arange(half_dim).astype(jnp.float32) / values.shape[-1]
    )
    angles = positions[:, None] * frequency[None, :]
    cosine = jnp.cos(angles)[:, None, :]
    sine_part = jnp.sin(angles)[:, None, :]
    first_half = values[..., :half_dim]
    second = values[..., half_dim:]
    return jnp.concatenate(
        [first_half * cosine - second * sine_part, second * cosine + first_half * sine_part],
        axis=-1,
    )


def body(
    hidden_in,
    norm_attn,
    w_query,
    w_key,
    w_value,
    w_out,
    prefix_cache,
    page_table,
    group_of,
    suffix_len,
    norm_moe,
    expert_ids,
    expert_weights,
    w_gate,
    w_up,
    w_down,
):
    req_count = lax.axis_size("req")
    tp_count = lax.axis_size("tp")
    req_index = lax.axis_index("req")
    tp_index = lax.axis_index("tp")
    rows_here = hidden_in.shape[0]
    feature_cols = hidden_in.shape[1]
    heads_here = w_query.shape[1] // HD
    shared_head = tp_index // (tp_count // KVH)
    hidden = hidden_in.astype(jnp.float32)
    full_in = lax.all_gather(hidden_in, "tp", axis=1, tiled=True).astype(jnp.float32)
    sq_in = jnp.sum(full_in * full_in, axis=1)
    shard_piece = (full_in * lax.rsqrt(sq_in / D + EPSILON)[:, None] * norm_attn).astype(
        jnp.bfloat16
    )
    key_cols = lax.dynamic_slice_in_dim(w_key, shared_head * HD, HD, 1)
    value_cols = lax.dynamic_slice_in_dim(w_value, shared_head * HD, HD, 1)
    w_both = jnp.concatenate([key_cols, value_cols], axis=1)
    query_lin = jnp.dot(shard_piece, w_query, preferred_element_type=jnp.float32)
    pair_lin = jnp.dot(shard_piece, w_both, preferred_element_type=jnp.float32)
    positions = (PREFIX + jnp.arange(rows_here)).astype(jnp.float32)
    query_rot = rotate(query_lin.reshape(rows_here, heads_here, HD), positions).astype(jnp.bfloat16)
    key_suf = rotate(pair_lin[:, None, :HD], positions)[:, 0].astype(jnp.bfloat16)
    value_suf = pair_lin[:, HD:].astype(jnp.bfloat16)
    groups = page_table.shape[0]
    local_pages = prefix_cache.shape[0]
    page_rows = prefix_cache.shape[3]
    most_pages = min(local_pages // 2, 2 * page_table.shape[1] // req_count)
    my_group = group_of[req_index]
    owner_of = page_table // local_pages
    slot_of = page_table % local_pages
    owned_here = (owner_of == req_index).astype(jnp.int32)
    slot_rank = jnp.cumsum(owned_here, axis=1) - 1
    picker = (
        owned_here[:, :, None, None]
        * (slot_rank[:, :, None, None] == jnp.arange(most_pages)[None, None, :, None])
        * (slot_of[:, :, None, None] == jnp.arange(local_pages)[None, None, None, :])
    )
    picker = jnp.sum(picker, axis=1).astype(jnp.float32)
    peer_group = (group_of[:, None] == jnp.arange(groups)[None, :]).astype(jnp.float32)
    choose = jnp.einsum("qg,grs->qrs", peer_group, picker).astype(jnp.bfloat16)
    pair_size = tp_count // KVH
    half_index = tp_index % pair_size
    half_rows = page_rows // pair_size
    local_head = lax.dynamic_index_in_dim(prefix_cache, shared_head, axis=2, keepdims=False)
    local_half = lax.dynamic_slice_in_dim(local_head, half_index * half_rows, half_rows, 2)
    flat_cache = local_half.reshape(local_pages, -1)
    outgoing = jnp.einsum(
        "qrs,sx->qrx", choose, flat_cache, preferred_element_type=jnp.float32
    ).astype(jnp.bfloat16)
    incoming = lax.all_to_all(
        outgoing.reshape(req_count, most_pages, 2, half_rows, HD),
        "req",
        split_axis=0,
        concat_axis=0,
        tiled=True,
    )
    my_owners = lax.dynamic_index_in_dim(owner_of, my_group, axis=0, keepdims=False)
    page_count = jnp.sum(my_owners[None, :] == jnp.arange(req_count)[:, None], axis=1)
    live_count = page_table.shape[1] // most_pages
    owner_live = page_count > 0
    live_rank = jnp.cumsum(owner_live.astype(jnp.int32)) - 1
    live_pick = (live_rank[None, :] == jnp.arange(live_count)[:, None]) & owner_live[None, :]
    live_owner = jnp.sum(jnp.where(live_pick, jnp.arange(req_count)[None, :], 0), axis=1)
    compact = jnp.take(incoming, live_owner, axis=0)
    keys_pre = compact[:, :, 0]
    values_pre = compact[:, :, 1]
    pair_perm = [(i, i ^ 1) for i in range(tp_count)]
    partner_query = lax.ppermute(query_rot, "tp", pair_perm)
    query_six = jnp.concatenate([query_rot, partner_query], axis=1)
    key_total = live_count * most_pages * half_rows
    block_len = math.gcd(key_total, 2048)
    block_count = key_total // block_len
    score_scale = 1.0 / math.sqrt(HD)
    scores = (
        jnp.einsum("thd,jd->thj", query_rot, key_suf, preferred_element_type=jnp.float32)
        * score_scale
    )
    causal = jnp.arange(rows_here)[:, None] >= jnp.arange(rows_here)[None, :]
    scores = jnp.where(causal[:, None, :], scores, MASKED)
    suf_max = jnp.max(scores, axis=2)
    weights = jnp.exp(scores - suf_max[:, :, None])
    suf_sum = jnp.sum(weights, axis=2)
    suf_weighted = jnp.einsum(
        "thj,jd->thd", weights.astype(jnp.bfloat16), value_suf, preferred_element_type=jnp.float32
    )

    def absorb(running, block_parts):
        old_max, old_sum, old_weighted = running
        key_block, value_block = block_parts
        block_scores = (
            jnp.einsum("thd,kd->thk", query_six, key_block, preferred_element_type=jnp.float32)
            * score_scale
        )
        new_max = jnp.maximum(old_max, jnp.max(block_scores, axis=2))
        rescale = jnp.exp(old_max - new_max)
        block_weights = jnp.exp(block_scores - new_max[:, :, None])
        new_sum = old_sum * rescale + jnp.sum(block_weights, axis=2)
        new_weighted = old_weighted * rescale[:, :, None] + jnp.einsum(
            "thk,kd->thd",
            block_weights.astype(jnp.bfloat16),
            value_block,
            preferred_element_type=jnp.float32,
        )
        return ((new_max, new_sum, new_weighted), None)

    block_inputs = (
        keys_pre.reshape(block_count, block_len, HD),
        values_pre.reshape(block_count, block_len, HD),
    )
    gate_full = lax.all_gather(w_gate[0], "tp", axis=1, tiled=True)
    up_full = lax.all_gather(w_up[0], "tp", axis=1, tiled=True)
    expert_count = w_gate.shape[0] * req_count
    capacity = 3 * rows_here * TOP // (2 * expert_count)
    sub = capacity // tp_count
    onehot_exp = (
        (expert_ids[:, :, None] == jnp.arange(expert_count)[None, None, :])
        .astype(jnp.int32)
        .reshape(rows_here * TOP, expert_count)
    )
    pair_rank = jnp.sum(jnp.cumsum(onehot_exp, axis=0) * onehot_exp, axis=1) - 1
    mine = (pair_rank // sub) == tp_index
    send_pos = expert_ids.reshape(-1) * sub + pair_rank % sub
    pair_token = jnp.arange(rows_here * TOP) // TOP
    slot_match = (send_pos[None, :] == jnp.arange(expert_count * sub)[:, None]) & mine[None, :]
    slot_token = jnp.sum(jnp.where(slot_match, pair_token[None, :], 0), axis=1)
    slot_token, send_pos, mine, norm_moe, block_inputs = lax.optimization_barrier(
        (slot_token, send_pos, mine, norm_moe, block_inputs)
    )
    six = 2 * heads_here
    start_state = (
        jnp.full((rows_here, six), MASKED, jnp.float32),
        jnp.zeros((rows_here, six), jnp.float32),
        jnp.zeros((rows_here, six, HD), jnp.float32),
    )
    (pre_max, pre_sum, pre_weighted), _ = lax.scan(absorb, start_state, block_inputs)
    gate_full, up_full, pre_max, pre_sum, pre_weighted = lax.optimization_barrier(
        (gate_full, up_full, pre_max, pre_sum, pre_weighted)
    )
    back = lax.ppermute(
        (pre_max[:, heads_here:], pre_sum[:, heads_here:], pre_weighted[:, heads_here:]),
        "tp",
        pair_perm,
    )
    parts = (
        (suf_max, suf_sum, suf_weighted),
        (pre_max[:, :heads_here], pre_sum[:, :heads_here], pre_weighted[:, :heads_here]),
        back,
    )
    row_max = jnp.maximum(jnp.maximum(parts[0][0], parts[1][0]), parts[2][0])
    row_sum = jnp.zeros_like(row_max)
    weighted = jnp.zeros_like(suf_weighted)
    for part_max, part_sum, part_weighted in parts:
        rescale = jnp.exp(part_max - row_max)
        row_sum = row_sum + part_sum * rescale
        weighted = weighted + part_weighted * rescale[:, :, None]
    attention = (
        (weighted / row_sum[:, :, None]).astype(jnp.bfloat16).reshape(rows_here, heads_here * HD)
    )
    proj_part = jnp.dot(attention, w_out, preferred_element_type=jnp.float32)
    attn_sum = lax.psum(proj_part.astype(jnp.bfloat16), "tp")
    down_local, attn_sum = lax.optimization_barrier((w_down[0], attn_sum))
    down_full = lax.all_gather(down_local, "tp", axis=0, tiled=True)
    attn_full = attn_sum.astype(jnp.float32)
    residual_full = full_in + attn_full
    sq_mid = jnp.sum(residual_full * residual_full, axis=1)
    full_rows = (residual_full * lax.rsqrt(sq_mid / D + EPSILON)[:, None] * norm_moe).astype(
        jnp.bfloat16
    )
    residual = lax.dynamic_slice_in_dim(residual_full, tp_index * feature_cols, feature_cols, 1)
    outgoing_rows = jnp.take(full_rows, slot_token, axis=0).reshape(
        req_count, sub, full_rows.shape[1]
    )
    rows_in = lax.all_to_all(outgoing_rows, "req", split_axis=0, concat_axis=0, tiled=True)
    src_count, item_count, width_all = rows_in.shape
    flat_rows = rows_in.reshape(src_count * item_count, width_all)
    gate_lin = jnp.dot(flat_rows, gate_full, preferred_element_type=jnp.float32)
    up_lin = jnp.dot(flat_rows, up_full, preferred_element_type=jnp.float32)
    hidden_act = (jnp.maximum(gate_lin, 0.0) * up_lin).astype(jnp.bfloat16)
    block = hidden_act.shape[1] // tp_count
    down_parts = jnp.einsum(
        "rqf,qfd->qrd",
        hidden_act.reshape(-1, tp_count, block),
        down_full.reshape(tp_count, block, width_all),
        preferred_element_type=jnp.float32,
    ).astype(jnp.bfloat16)
    expert_out = jnp.sum(down_parts.astype(jnp.float32), axis=0).astype(jnp.bfloat16)
    to_slices = expert_out.reshape(src_count, item_count, tp_count, feature_cols)
    to_slices = jnp.transpose(to_slices, (0, 2, 1, 3)).reshape(-1, item_count, feature_cols)
    returned = lax.all_to_all(to_slices, ("req", "tp"), split_axis=0, concat_axis=0, tiled=True)
    flat_back = returned.reshape(-1, feature_cols)
    slot_all = expert_ids * capacity + pair_rank.reshape(rows_here, TOP)
    slot_hit = slot_all[:, :, None] == jnp.arange(flat_back.shape[0])
    combine = jnp.sum(jnp.where(slot_hit, expert_weights[:, :, None], 0.0), axis=1)
    moe_part = jnp.dot(
        combine,
        flat_back.astype(jnp.float32),
        precision=lax.Precision.HIGHEST,
        preferred_element_type=jnp.float32,
    )
    layer_out = residual + moe_part
    live_rows = jnp.arange(rows_here) < suffix_len[0]
    return jnp.where(live_rows[:, None], layer_out, 0.0).astype(jnp.bfloat16)


def solution(mesh):
    in_specs = (
        P("req", "tp"),
        P(),
        P(None, "tp"),
        P(),
        P(),
        P("tp", None),
        P("req", None, None, None, None),
        P(),
        P(),
        P("req"),
        P(),
        P("req", None),
        P("req", None),
        P("req", None, "tp"),
        P("req", None, "tp"),
        P("req", "tp", None),
    )
    out_specs = P("req", "tp")
    return jax.shard_map(body, mesh=mesh, in_specs=in_specs, out_specs=out_specs, check_vma=False)
```

```python
import math

import jax
import jax.numpy as jnp
from jax import lax
from jax.sharding import PartitionSpec as P

D = 1536
KVH = 2
HD = 128
TOP = 4
PREFIX = 8192


EPSILON = 1e-06
ROPE_BASE = 1000000.0
MASKED = -1e30


def rotate(values, positions):
    half_dim = values.shape[-1] // 2
    frequency = jnp.power(
        ROPE_BASE, -2.0 * jnp.arange(half_dim).astype(jnp.float32) / values.shape[-1]
    )
    angles = positions[:, None] * frequency[None, :]
    cosine = jnp.cos(angles)[:, None, :]
    sine_part = jnp.sin(angles)[:, None, :]
    first_half = values[..., :half_dim]
    second = values[..., half_dim:]
    return jnp.concatenate(
        [first_half * cosine - second * sine_part, second * cosine + first_half * sine_part],
        axis=-1,
    )


def body(
    hidden_in,
    norm_attn,
    w_query,
    w_key,
    w_value,
    w_out,
    prefix_cache,
    page_table,
    group_of,
    suffix_len,
    norm_moe,
    expert_ids,
    expert_weights,
    w_gate,
    w_up,
    w_down,
):
    req_count = lax.axis_size("req")
    tp_count = lax.axis_size("tp")
    req_index = lax.axis_index("req")
    tp_index = lax.axis_index("tp")
    rows_here = hidden_in.shape[0]
    feature_cols = hidden_in.shape[1]
    heads_here = w_query.shape[1] // HD
    shared_head = tp_index // (tp_count // KVH)
    hidden = hidden_in.astype(jnp.float32)
    full_in = lax.all_gather(hidden_in, "tp", axis=1, tiled=True).astype(jnp.float32)
    sq_in = jnp.sum(full_in * full_in, axis=1)
    shard_piece = (full_in * lax.rsqrt(sq_in / D + EPSILON)[:, None] * norm_attn).astype(
        jnp.bfloat16
    )
    key_cols = lax.dynamic_slice_in_dim(w_key, shared_head * HD, HD, 1)
    value_cols = lax.dynamic_slice_in_dim(w_value, shared_head * HD, HD, 1)
    w_both = jnp.concatenate([key_cols, value_cols], axis=1)
    query_lin = jnp.dot(shard_piece, w_query, preferred_element_type=jnp.float32)
    pair_lin = jnp.dot(shard_piece, w_both, preferred_element_type=jnp.float32)
    positions = (PREFIX + jnp.arange(rows_here)).astype(jnp.float32)
    query_rot = rotate(query_lin.reshape(rows_here, heads_here, HD), positions).astype(jnp.bfloat16)
    key_suf = rotate(pair_lin[:, None, :HD], positions)[:, 0].astype(jnp.bfloat16)
    value_suf = pair_lin[:, HD:].astype(jnp.bfloat16)
    groups = page_table.shape[0]
    local_pages = prefix_cache.shape[0]
    page_rows = prefix_cache.shape[3]
    most_pages = min(local_pages // 2, 2 * page_table.shape[1] // req_count)
    my_group = group_of[req_index]
    owner_of = page_table // local_pages
    slot_of = page_table % local_pages
    owned_here = (owner_of == req_index).astype(jnp.int32)
    slot_rank = jnp.cumsum(owned_here, axis=1) - 1
    picker = (
        owned_here[:, :, None, None]
        * (slot_rank[:, :, None, None] == jnp.arange(most_pages)[None, None, :, None])
        * (slot_of[:, :, None, None] == jnp.arange(local_pages)[None, None, None, :])
    )
    picker = jnp.sum(picker, axis=1).astype(jnp.float32)
    peer_group = (group_of[:, None] == jnp.arange(groups)[None, :]).astype(jnp.float32)
    choose = jnp.einsum("qg,grs->qrs", peer_group, picker).astype(jnp.bfloat16)
    pair_size = tp_count // KVH
    half_index = tp_index % pair_size
    half_rows = page_rows // pair_size
    local_head = lax.dynamic_index_in_dim(prefix_cache, shared_head, axis=2, keepdims=False)
    local_half = lax.dynamic_slice_in_dim(local_head, half_index * half_rows, half_rows, 2)
    flat_cache = local_half.reshape(local_pages, -1)
    outgoing = jnp.einsum(
        "qrs,sx->qrx", choose, flat_cache, preferred_element_type=jnp.float32
    ).astype(jnp.bfloat16)
    incoming = lax.all_to_all(
        outgoing.reshape(req_count, most_pages, 2, half_rows, HD),
        "req",
        split_axis=0,
        concat_axis=0,
        tiled=True,
    )
    my_owners = lax.dynamic_index_in_dim(owner_of, my_group, axis=0, keepdims=False)
    page_count = jnp.sum(my_owners[None, :] == jnp.arange(req_count)[:, None], axis=1)
    live_count = page_table.shape[1] // most_pages
    owner_live = page_count > 0
    live_rank = jnp.cumsum(owner_live.astype(jnp.int32)) - 1
    live_pick = (live_rank[None, :] == jnp.arange(live_count)[:, None]) & owner_live[None, :]
    live_owner = jnp.sum(jnp.where(live_pick, jnp.arange(req_count)[None, :], 0), axis=1)
    compact = jnp.take(incoming, live_owner, axis=0)
    keys_pre = compact[:, :, 0]
    values_pre = compact[:, :, 1]
    pair_perm = [(i, i ^ 1) for i in range(tp_count)]
    partner_query = lax.ppermute(query_rot, "tp", pair_perm)
    query_six = jnp.concatenate([query_rot, partner_query], axis=1)
    key_total = live_count * most_pages * half_rows
    block_len = math.gcd(key_total, 2048)
    block_count = key_total // block_len
    score_scale = 1.0 / math.sqrt(HD)
    scores = (
        jnp.einsum("thd,jd->thj", query_rot, key_suf, preferred_element_type=jnp.float32)
        * score_scale
    )
    causal = jnp.arange(rows_here)[:, None] >= jnp.arange(rows_here)[None, :]
    scores = jnp.where(causal[:, None, :], scores, MASKED)
    suf_max = jnp.max(scores, axis=2)
    weights = jnp.exp(scores - suf_max[:, :, None])
    suf_sum = jnp.sum(weights, axis=2)
    suf_weighted = jnp.einsum(
        "thj,jd->thd", weights.astype(jnp.bfloat16), value_suf, preferred_element_type=jnp.float32
    )

    def absorb(running, block_parts):
        old_max, old_sum, old_weighted = running
        key_block, value_block = block_parts
        block_scores = (
            jnp.einsum("thd,kd->thk", query_six, key_block, preferred_element_type=jnp.float32)
            * score_scale
        )
        new_max = jnp.maximum(old_max, jnp.max(block_scores, axis=2))
        rescale = jnp.exp(old_max - new_max)
        block_weights = jnp.exp(block_scores - new_max[:, :, None])
        new_sum = old_sum * rescale + jnp.sum(block_weights, axis=2)
        new_weighted = old_weighted * rescale[:, :, None] + jnp.einsum(
            "thk,kd->thd",
            block_weights.astype(jnp.bfloat16),
            value_block,
            preferred_element_type=jnp.float32,
        )
        return ((new_max, new_sum, new_weighted), None)

    block_inputs = (
        keys_pre.reshape(block_count, block_len, HD),
        values_pre.reshape(block_count, block_len, HD),
    )
    gate_full = lax.all_gather(w_gate[0], "tp", axis=1, tiled=True)
    up_full = lax.all_gather(w_up[0], "tp", axis=1, tiled=True)
    expert_count = w_gate.shape[0] * req_count
    capacity = 3 * rows_here * TOP // (2 * expert_count)
    sub = capacity // tp_count
    onehot_exp = (
        (expert_ids[:, :, None] == jnp.arange(expert_count)[None, None, :])
        .astype(jnp.int32)
        .reshape(rows_here * TOP, expert_count)
    )
    pair_rank = jnp.sum(jnp.cumsum(onehot_exp, axis=0) * onehot_exp, axis=1) - 1
    mine = (pair_rank // sub) == tp_index
    send_pos = expert_ids.reshape(-1) * sub + pair_rank % sub
    pair_token = jnp.arange(rows_here * TOP) // TOP
    slot_global = expert_ids.reshape(-1) * capacity + pair_rank
    slot_match = slot_global[None, :] == jnp.arange(expert_count * capacity)[:, None]
    slot_token = jnp.sum(jnp.where(slot_match, pair_token[None, :], 0), axis=1)
    slot_token, send_pos, mine, norm_moe, block_inputs = lax.optimization_barrier(
        (slot_token, send_pos, mine, norm_moe, block_inputs)
    )
    six = 2 * heads_here
    start_state = (
        jnp.full((rows_here, six), MASKED, jnp.float32),
        jnp.zeros((rows_here, six), jnp.float32),
        jnp.zeros((rows_here, six, HD), jnp.float32),
    )
    (pre_max, pre_sum, pre_weighted), _ = lax.scan(absorb, start_state, block_inputs)
    gate_full, up_full, pre_max, pre_sum, pre_weighted = lax.optimization_barrier(
        (gate_full, up_full, pre_max, pre_sum, pre_weighted)
    )
    back = lax.ppermute(
        (pre_max[:, heads_here:], pre_sum[:, heads_here:], pre_weighted[:, heads_here:]),
        "tp",
        pair_perm,
    )
    parts = (
        (suf_max, suf_sum, suf_weighted),
        (pre_max[:, :heads_here], pre_sum[:, :heads_here], pre_weighted[:, :heads_here]),
        back,
    )
    row_max = jnp.maximum(jnp.maximum(parts[0][0], parts[1][0]), parts[2][0])
    row_sum = jnp.zeros_like(row_max)
    weighted = jnp.zeros_like(suf_weighted)
    for part_max, part_sum, part_weighted in parts:
        rescale = jnp.exp(part_max - row_max)
        row_sum = row_sum + part_sum * rescale
        weighted = weighted + part_weighted * rescale[:, :, None]
    attention = (
        (weighted / row_sum[:, :, None]).astype(jnp.bfloat16).reshape(rows_here, heads_here * HD)
    )
    proj_part = jnp.dot(attention, w_out, preferred_element_type=jnp.float32)
    attn_sum = lax.psum(proj_part.astype(jnp.bfloat16), "tp")
    down_local, attn_sum = lax.optimization_barrier((w_down[0], attn_sum))
    down_full = lax.all_gather(down_local, "tp", axis=0, tiled=True)
    attn_full = attn_sum.astype(jnp.float32)
    residual_full = full_in + attn_full
    sq_mid = jnp.sum(residual_full * residual_full, axis=1)
    full_rows = (residual_full * lax.rsqrt(sq_mid / D + EPSILON)[:, None] * norm_moe).astype(
        jnp.bfloat16
    )
    residual = lax.dynamic_slice_in_dim(residual_full, tp_index * feature_cols, feature_cols, 1)
    my_cols = lax.dynamic_slice_in_dim(full_rows, tp_index * feature_cols, feature_cols, 1)
    outgoing_rows = jnp.take(my_cols, slot_token, axis=0).reshape(-1, sub, feature_cols)
    pieces_in = lax.all_to_all(outgoing_rows, ("req", "tp"), split_axis=0, concat_axis=0, tiled=True)
    pieces_in = pieces_in.reshape(req_count, tp_count, sub, feature_cols)
    rows_in = jnp.transpose(pieces_in, (0, 2, 1, 3)).reshape(req_count, sub, -1)
    src_count, item_count, width_all = rows_in.shape
    flat_rows = rows_in.reshape(src_count * item_count, width_all)
    gate_lin = jnp.dot(flat_rows, gate_full, preferred_element_type=jnp.float32)
    up_lin = jnp.dot(flat_rows, up_full, preferred_element_type=jnp.float32)
    hidden_act = (jnp.maximum(gate_lin, 0.0) * up_lin).astype(jnp.bfloat16)
    block = hidden_act.shape[1] // tp_count
    down_parts = jnp.einsum(
        "rqf,qfd->qrd",
        hidden_act.reshape(-1, tp_count, block),
        down_full.reshape(tp_count, block, width_all),
        preferred_element_type=jnp.float32,
    ).astype(jnp.bfloat16)
    expert_out = jnp.sum(down_parts.astype(jnp.float32), axis=0).astype(jnp.bfloat16)
    to_slices = expert_out.reshape(src_count, item_count, tp_count, feature_cols)
    to_slices = jnp.transpose(to_slices, (0, 2, 1, 3)).reshape(-1, item_count, feature_cols)
    returned = lax.all_to_all(to_slices, ("req", "tp"), split_axis=0, concat_axis=0, tiled=True)
    flat_back = returned.reshape(-1, feature_cols)
    slot_all = expert_ids * capacity + pair_rank.reshape(rows_here, TOP)
    slot_hit = slot_all[:, :, None] == jnp.arange(flat_back.shape[0])
    combine = jnp.sum(jnp.where(slot_hit, expert_weights[:, :, None], 0.0), axis=1)
    moe_part = jnp.dot(
        combine,
        flat_back.astype(jnp.float32),
        precision=lax.Precision.HIGHEST,
        preferred_element_type=jnp.float32,
    )
    layer_out = residual + moe_part
    live_rows = jnp.arange(rows_here) < suffix_len[0]
    return jnp.where(live_rows[:, None], layer_out, 0.0).astype(jnp.bfloat16)


def solution(mesh):
    in_specs = (
        P("req", "tp"),
        P(),
        P(None, "tp"),
        P(),
        P(),
        P("tp", None),
        P("req", None, None, None, None),
        P(),
        P(),
        P("req"),
        P(),
        P("req", None),
        P("req", None),
        P("req", None, "tp"),
        P("req", None, "tp"),
        P("req", "tp", None),
    )
    out_specs = P("req", "tp")
    return jax.shard_map(body, mesh=mesh, in_specs=in_specs, out_specs=out_specs, check_vma=False)
```

```python
import math

import jax
import jax.numpy as jnp
from jax import lax
from jax.sharding import PartitionSpec as P

D = 1536
KVH = 2
HD = 128
TOP = 4
PREFIX = 8192


EPSILON = 1e-06
ROPE_BASE = 1000000.0
MASKED = -1e30


def rotate(values, positions):
    half_dim = values.shape[-1] // 2
    frequency = jnp.power(
        ROPE_BASE, -2.0 * jnp.arange(half_dim).astype(jnp.float32) / values.shape[-1]
    )
    angles = positions[:, None] * frequency[None, :]
    cosine = jnp.cos(angles)[:, None, :]
    sine_part = jnp.sin(angles)[:, None, :]
    first_half = values[..., :half_dim]
    second = values[..., half_dim:]
    return jnp.concatenate(
        [first_half * cosine - second * sine_part, second * cosine + first_half * sine_part],
        axis=-1,
    )


def body(
    hidden_in,
    norm_attn,
    w_query,
    w_key,
    w_value,
    w_out,
    prefix_cache,
    page_table,
    group_of,
    suffix_len,
    norm_moe,
    expert_ids,
    expert_weights,
    w_gate,
    w_up,
    w_down,
):
    req_count = lax.axis_size("req")
    tp_count = lax.axis_size("tp")
    req_index = lax.axis_index("req")
    tp_index = lax.axis_index("tp")
    rows_here = hidden_in.shape[0]
    feature_cols = hidden_in.shape[1]
    heads_here = w_query.shape[1] // HD
    shared_head = tp_index // (tp_count // KVH)
    hidden = hidden_in.astype(jnp.float32)
    full_in = lax.all_gather(hidden_in, "tp", axis=1, tiled=True).astype(jnp.float32)
    sq_in = jnp.sum(full_in * full_in, axis=1)
    shard_piece = (full_in * lax.rsqrt(sq_in / D + EPSILON)[:, None] * norm_attn).astype(
        jnp.bfloat16
    )
    key_cols = lax.dynamic_slice_in_dim(w_key, shared_head * HD, HD, 1)
    value_cols = lax.dynamic_slice_in_dim(w_value, shared_head * HD, HD, 1)
    w_both = jnp.concatenate([key_cols, value_cols], axis=1)
    query_lin = jnp.dot(shard_piece, w_query, preferred_element_type=jnp.float32)
    pair_lin = jnp.dot(shard_piece, w_both, preferred_element_type=jnp.float32)
    positions = (PREFIX + jnp.arange(rows_here)).astype(jnp.float32)
    query_rot = rotate(query_lin.reshape(rows_here, heads_here, HD), positions).astype(jnp.bfloat16)
    key_suf = rotate(pair_lin[:, None, :HD], positions)[:, 0].astype(jnp.bfloat16)
    value_suf = pair_lin[:, HD:].astype(jnp.bfloat16)
    groups = page_table.shape[0]
    local_pages = prefix_cache.shape[0]
    page_rows = prefix_cache.shape[3]
    most_pages = min(local_pages // 2, 2 * page_table.shape[1] // req_count)
    my_group = group_of[req_index]
    owner_of = page_table // local_pages
    slot_of = page_table % local_pages
    owned_here = (owner_of == req_index).astype(jnp.int32)
    slot_rank = jnp.cumsum(owned_here, axis=1) - 1
    picker = (
        owned_here[:, :, None, None]
        * (slot_rank[:, :, None, None] == jnp.arange(most_pages)[None, None, :, None])
        * (slot_of[:, :, None, None] == jnp.arange(local_pages)[None, None, None, :])
    )
    picker = jnp.sum(picker, axis=1).astype(jnp.float32)
    peer_group = (group_of[:, None] == jnp.arange(groups)[None, :]).astype(jnp.float32)
    choose = jnp.einsum("qg,grs->qrs", peer_group, picker).astype(jnp.bfloat16)
    pair_size = tp_count // KVH
    half_index = tp_index % pair_size
    half_rows = page_rows // pair_size
    local_head = lax.dynamic_index_in_dim(prefix_cache, shared_head, axis=2, keepdims=False)
    local_half = lax.dynamic_slice_in_dim(local_head, half_index * half_rows, half_rows, 2)
    flat_cache = local_half.reshape(local_pages, -1)
    outgoing = jnp.einsum(
        "qrs,sx->qrx", choose, flat_cache, preferred_element_type=jnp.float32
    ).astype(jnp.bfloat16)
    incoming = lax.all_to_all(
        outgoing.reshape(req_count, most_pages, 2, half_rows, HD),
        "req",
        split_axis=0,
        concat_axis=0,
        tiled=True,
    )
    my_owners = lax.dynamic_index_in_dim(owner_of, my_group, axis=0, keepdims=False)
    page_count = jnp.sum(my_owners[None, :] == jnp.arange(req_count)[:, None], axis=1)
    live_count = page_table.shape[1] // most_pages
    owner_live = page_count > 0
    live_rank = jnp.cumsum(owner_live.astype(jnp.int32)) - 1
    live_pick = (live_rank[None, :] == jnp.arange(live_count)[:, None]) & owner_live[None, :]
    live_owner = jnp.sum(jnp.where(live_pick, jnp.arange(req_count)[None, :], 0), axis=1)
    compact = jnp.take(incoming, live_owner, axis=0)
    keys_pre = compact[:, :, 0]
    values_pre = compact[:, :, 1]
    pair_perm = [(i, i ^ 1) for i in range(tp_count)]
    partner_query = lax.ppermute(query_rot, "tp", pair_perm)
    query_six = jnp.concatenate([query_rot, partner_query], axis=1)
    key_total = live_count * most_pages * half_rows
    block_len = math.gcd(key_total, 2048)
    block_count = key_total // block_len
    score_scale = 1.0 / math.sqrt(HD)
    scores = (
        jnp.einsum("thd,jd->thj", query_rot, key_suf, preferred_element_type=jnp.float32)
        * score_scale
    )
    causal = jnp.arange(rows_here)[:, None] >= jnp.arange(rows_here)[None, :]
    scores = jnp.where(causal[:, None, :], scores, MASKED)
    suf_max = jnp.max(scores, axis=2)
    weights = jnp.exp(scores - suf_max[:, :, None])
    suf_sum = jnp.sum(weights, axis=2)
    suf_weighted = jnp.einsum(
        "thj,jd->thd", weights.astype(jnp.bfloat16), value_suf, preferred_element_type=jnp.float32
    )

    def absorb(running, block_parts):
        old_max, old_sum, old_weighted = running
        key_block, value_block = block_parts
        block_scores = (
            jnp.einsum("thd,kd->thk", query_six, key_block, preferred_element_type=jnp.float32)
            * score_scale
        )
        new_max = jnp.maximum(old_max, jnp.max(block_scores, axis=2))
        rescale = jnp.exp(old_max - new_max)
        block_weights = jnp.exp(block_scores - new_max[:, :, None])
        new_sum = old_sum * rescale + jnp.sum(block_weights, axis=2)
        new_weighted = old_weighted * rescale[:, :, None] + jnp.einsum(
            "thk,kd->thd",
            block_weights.astype(jnp.bfloat16),
            value_block,
            preferred_element_type=jnp.float32,
        )
        return ((new_max, new_sum, new_weighted), None)

    block_inputs = (
        keys_pre.reshape(block_count, block_len, HD),
        values_pre.reshape(block_count, block_len, HD),
    )
    gate_full = lax.all_gather(w_gate[0], "tp", axis=1, tiled=True)
    up_full = lax.all_gather(w_up[0], "tp", axis=1, tiled=True)
    expert_count = w_gate.shape[0] * req_count
    capacity = 3 * rows_here * TOP // (2 * expert_count)
    sub = capacity // tp_count
    onehot_exp = (
        (expert_ids[:, :, None] == jnp.arange(expert_count)[None, None, :])
        .astype(jnp.int32)
        .reshape(rows_here * TOP, expert_count)
    )
    pair_rank = jnp.sum(jnp.cumsum(onehot_exp, axis=0) * onehot_exp, axis=1) - 1
    mine = (pair_rank // sub) == tp_index
    send_pos = expert_ids.reshape(-1) * sub + pair_rank % sub
    pair_token = jnp.arange(rows_here * TOP) // TOP
    slot_match = (send_pos[None, :] == jnp.arange(expert_count * sub)[:, None]) & mine[None, :]
    slot_token = jnp.sum(jnp.where(slot_match, pair_token[None, :], 0), axis=1)
    slot_token, send_pos, mine, norm_moe, block_inputs = lax.optimization_barrier(
        (slot_token, send_pos, mine, norm_moe, block_inputs)
    )
    six = 2 * heads_here
    start_state = (
        jnp.full((rows_here, six), MASKED, jnp.float32),
        jnp.zeros((rows_here, six), jnp.float32),
        jnp.zeros((rows_here, six, HD), jnp.float32),
    )
    (pre_max, pre_sum, pre_weighted), _ = lax.scan(absorb, start_state, block_inputs)
    gate_full, up_full, pre_max, pre_sum, pre_weighted = lax.optimization_barrier(
        (gate_full, up_full, pre_max, pre_sum, pre_weighted)
    )
    back = lax.ppermute(
        (pre_max[:, heads_here:], pre_sum[:, heads_here:], pre_weighted[:, heads_here:]),
        "tp",
        pair_perm,
    )
    parts = (
        (suf_max, suf_sum, suf_weighted),
        (pre_max[:, :heads_here], pre_sum[:, :heads_here], pre_weighted[:, :heads_here]),
        back,
    )
    row_max = jnp.maximum(jnp.maximum(parts[0][0], parts[1][0]), parts[2][0])
    row_sum = jnp.zeros_like(row_max)
    weighted = jnp.zeros_like(suf_weighted)
    for part_max, part_sum, part_weighted in parts:
        rescale = jnp.exp(part_max - row_max)
        row_sum = row_sum + part_sum * rescale
        weighted = weighted + part_weighted * rescale[:, :, None]
    attention = (
        (weighted / row_sum[:, :, None]).astype(jnp.bfloat16).reshape(rows_here, heads_here * HD)
    )
    proj_part = jnp.dot(attention, w_out, preferred_element_type=jnp.float32)
    attn_part = lax.psum_scatter(
        proj_part.astype(jnp.bfloat16), "tp", scatter_dimension=1, tiled=True
    )
    attn_sum = lax.all_gather(attn_part, "tp", axis=1, tiled=True)
    down_local, attn_sum = lax.optimization_barrier((w_down[0], attn_sum))
    down_full = lax.all_gather(down_local, "tp", axis=0, tiled=True)
    attn_full = attn_sum.astype(jnp.float32)
    residual_full = full_in + attn_full
    sq_mid = jnp.sum(residual_full * residual_full, axis=1)
    full_rows = (residual_full * lax.rsqrt(sq_mid / D + EPSILON)[:, None] * norm_moe).astype(
        jnp.bfloat16
    )
    residual = lax.dynamic_slice_in_dim(residual_full, tp_index * feature_cols, feature_cols, 1)
    outgoing_rows = jnp.take(full_rows, slot_token, axis=0).reshape(
        req_count, sub, full_rows.shape[1]
    )
    rows_in = lax.all_to_all(outgoing_rows, "req", split_axis=0, concat_axis=0, tiled=True)
    src_count, item_count, width_all = rows_in.shape
    flat_rows = rows_in.reshape(src_count * item_count, width_all)
    gate_lin = jnp.dot(flat_rows, gate_full, preferred_element_type=jnp.float32)
    up_lin = jnp.dot(flat_rows, up_full, preferred_element_type=jnp.float32)
    hidden_act = (jnp.maximum(gate_lin, 0.0) * up_lin).astype(jnp.bfloat16)
    block = hidden_act.shape[1] // tp_count
    down_parts = jnp.einsum(
        "rqf,qfd->qrd",
        hidden_act.reshape(-1, tp_count, block),
        down_full.reshape(tp_count, block, width_all),
        preferred_element_type=jnp.float32,
    ).astype(jnp.bfloat16)
    expert_out = jnp.sum(down_parts.astype(jnp.float32), axis=0).astype(jnp.bfloat16)
    to_slices = expert_out.reshape(src_count, item_count, tp_count, feature_cols)
    to_slices = jnp.transpose(to_slices, (0, 2, 1, 3)).reshape(-1, item_count, feature_cols)
    returned = lax.all_to_all(to_slices, ("req", "tp"), split_axis=0, concat_axis=0, tiled=True)
    flat_back = returned.reshape(-1, feature_cols)
    slot_all = expert_ids * capacity + pair_rank.reshape(rows_here, TOP)
    slot_hit = slot_all[:, :, None] == jnp.arange(flat_back.shape[0])
    combine = jnp.sum(jnp.where(slot_hit, expert_weights[:, :, None], 0.0), axis=1)
    moe_part = jnp.dot(
        combine,
        flat_back.astype(jnp.float32),
        precision=lax.Precision.HIGHEST,
        preferred_element_type=jnp.float32,
    )
    layer_out = residual + moe_part
    live_rows = jnp.arange(rows_here) < suffix_len[0]
    return jnp.where(live_rows[:, None], layer_out, 0.0).astype(jnp.bfloat16)


def solution(mesh):
    in_specs = (
        P("req", "tp"),
        P(),
        P(None, "tp"),
        P(),
        P(),
        P("tp", None),
        P("req", None, None, None, None),
        P(),
        P(),
        P("req"),
        P(),
        P("req", None),
        P("req", None),
        P("req", None, "tp"),
        P("req", None, "tp"),
        P("req", "tp", None),
    )
    out_specs = P("req", "tp")
    return jax.shard_map(body, mesh=mesh, in_specs=in_specs, out_specs=out_specs, check_vma=False)
```
